32 devices in a mesh: dp: 8 (over z, y), mp: 4 (over x, core).
Axes of the slice: x: 2, y: 2, z: 4, core: 2. Of those that a mesh axis runs over, the one named last changes fastest.
Arguments:
- hidden: bfloat16 [4096, 8192], P('dp', 'mp'), may hold values from -64 to 64
- queries: bfloat16 [4096, 4096], P('dp', 'mp'), may hold values from -512 to 512
- upstream: bfloat16 [4096, 4096], P('dp', 'mp'), may hold values from -6 to 6
- key_weight: bfloat16 [8192, 512], P(None, 'mp'), may hold values from -1 to 1
- value_weight: bfloat16 [8192, 512], P(None, 'mp'), may hold values from -0.0625 to 0.0625
- lengths: int32 [8, 8], replicated, may hold values from 0 to 64, as said below
- advantage: float32 [8, 8], replicated, may hold values from -4 to 4
Outputs:
- attention_out: bfloat16 [2048, 4096], P('dp', 'mp')
- key_grad: float32 [8192, 512], P('dp', 'mp')
- value_grad: float32 [8192, 512], P('dp', 'mp')
The draws below stay inside these ranges and needn't reach their ends.
Inputs may be any that keep to these rules, and one draw needn't show every extreme that they name: `lengths`: each rollout device fills its slots from slot 0; a used slot holds 33 to 64 tokens, later slots hold 0. Devices come in aligned groups of four; in each, the second or the third device is heavy and uses 6 to 8 slots; every other device uses one slot plus one for each neighbour that exists and is not heavy. One device's responses total at most 512 tokens and some device holds exactly 512; under the learner rule a learner receives at most 256 tokens and some learner exactly 256, and at most 128 tokens go from one device to one neighbour, exactly 128 from some device.
All inputs are finite; a program needn't handle non-finite values.
Results may differ from the reference program's by a relative error of at most 0.0082.
Values may be sent and summed in bfloat16 or wider, within the bound.
A program may use at most 128 MiB of HBM per device.

```python
import math
import jax
import jax.numpy as jnp
from jax import lax

D = 8192
QH = 32
KVH = 4
HD = 128
RESP = 8
LMAX = 64
CAP_R = 512
CAP_L = 256
ROWS_R = 4096
ROWS_L = 2048
N_DP = 8


def draw_lengths(key, part):
    base = jax.random.fold_in(key, 11)
    streams = jax.random.split(base, 6)
    device_total = ROWS_L // CAP_L
    group_total = device_total // 4
    heavy_place = jax.random.randint(streams[0], (group_total,), 1, 3)
    group_ids = jnp.arange(group_total)
    heavy_place = jnp.where(group_ids == 0, 2, jnp.where(group_ids == group_total - 1, 1, heavy_place))
    extra_count = jax.random.randint(streams[1], (group_total,), 2, 5)
    full_group = jax.random.randint(streams[4], (), 0, group_total)
    drawn = jax.random.randint(streams[5], (device_total, RESP), LMAX // 2 + 1, LMAX + 1)
    devices = jnp.arange(device_total)
    groups = devices // 4
    places = devices % 4
    heavy_flag = places == heavy_place[groups]
    forced = groups == full_group
    left_heavy = jnp.concatenate([jnp.zeros((1,), bool), heavy_flag[:-1]])
    right_heavy = jnp.concatenate([heavy_flag[1:], jnp.zeros((1,), bool)])
    has_left = devices > 0
    has_right = devices < device_total - 1
    light_left = (has_left & jnp.logical_not(left_heavy)).astype(jnp.int32)
    light_right = (has_right & jnp.logical_not(right_heavy)).astype(jnp.int32)
    extra_here = jnp.where(forced, 4, extra_count[groups])
    used_slots = jnp.where(heavy_flag, 4 + extra_here, 1 + light_left + light_right)
    slot_ids = jnp.arange(RESP)[None, :]
    drawn = jnp.where((heavy_flag & forced)[:, None], LMAX, drawn)
    lengths = jnp.where(slot_ids < used_slots[:, None], drawn, 0)
    return lengths.astype(jnp.int32)


def align_tables(key):
    base = jax.random.fold_in(key, 23)
    streams = jax.random.split(base, 4)
    weight = jnp.clip(jax.random.normal(streams[3], (D, KVH * HD), jnp.float32), -3.0, 3.0) * D ** (-0.5)
    return weight


def draw_key_weight(key, part):
    weight = align_tables(key)
    return weight.astype(jnp.bfloat16)


def draw_queries(key, part):
    streams = jax.random.split(jax.random.fold_in(key, 31), 1)
    values = jnp.clip(jax.random.normal(streams[0], (ROWS_R, QH * HD), jnp.float32), -6.0, 6.0)
    return values.astype(jnp.bfloat16)


def draw_hidden(key, part):
    streams = jax.random.split(jax.random.fold_in(key, 41), 3)
    row_scale = jnp.exp(jax.random.uniform(streams[0], (ROWS_R, 1), jnp.float32) * math.log(10.0))
    column_scale = jnp.exp(jax.random.uniform(streams[1], (1, D), jnp.float32) * math.log(10.0))
    noise = jnp.clip(jax.random.normal(streams[2], (ROWS_R, D), jnp.float32), -6.0, 6.0)
    values = noise * row_scale * column_scale * 0.1
    return values.astype(jnp.bfloat16)


def block_levels(stream_key, extent, shards, low, high):
    gain = 1.0
    for position, blocks in shards:
        draws = jax.random.uniform(jax.random.fold_in(jax.random.fold_in(stream_key, 6), position), (blocks,), jnp.float32, low / len(shards), high / len(shards))
        gain = gain * jnp.repeat(jnp.exp(draws), extent[position] // blocks).reshape((-1,) + (1,) * (len(extent) - 1 - position))
    return gain


def centred(key, shape, scale, limit, cuts=(), kind=jnp.bfloat16):
    array = jax.random.normal(key, shape, jnp.float32) * scale
    if len(cuts) > 0:
        array = block_levels(key, shape, cuts, -0.22, 0.18) * array
    return jnp.clip(array, min=-limit, max=limit).astype(kind)


def setup_inputs(seed: int = 0) -> dict:
    seeds = jax.random.split(jax.random.key(seed), 8)
    hidden = draw_hidden(jax.random.fold_in(seeds[7], 71), 0)
    queries = draw_queries(jax.random.fold_in(seeds[7], 71), 0)
    upstream = centred(seeds[2], (ROWS_R, QH * HD), 1.0, 6.0, ((0, 8), (1, 4)))
    key_weight = draw_key_weight(jax.random.fold_in(seeds[7], 71), 0)
    value_weight = centred(seeds[4], (D, KVH * HD), D ** -0.5, 0.0625, ((1, 4),))
    lengths = draw_lengths(jax.random.fold_in(seeds[7], 71), 0)
    advantage = centred(seeds[6], (N_DP, RESP), 1.0, 4.0, (), jnp.float32)
    return dict(hidden=hidden, queries=queries, upstream=upstream, key_weight=key_weight, value_weight=value_weight, lengths=lengths, advantage=advantage)


epsilon = 1e-06
masked_score = -1e+30

def derive_learner(lengths):
    device_total = lengths.shape[0]
    slot_total = lengths.shape[1]
    used_slots = lax.optimization_barrier(jnp.sum((lengths > 0).astype(jnp.int32), axis=1)).astype(jnp.int32)
    heavy_flag = used_slots >= 6
    devices = jnp.arange(device_total, dtype=jnp.int32)
    left_heavy = jnp.concatenate([jnp.zeros((1,), bool), heavy_flag[:-1]])
    light_left = ((devices > 0) & jnp.logical_not(left_heavy)).astype(jnp.int32)
    sent_left = jnp.where(heavy_flag, (used_slots - 4) // 2, light_left).astype(jnp.int32)
    kept_count = jnp.where(heavy_flag, 4, 1).astype(jnp.int32)
    slot_ids = jnp.arange(slot_total, dtype=jnp.int32)[None, :]
    slot_moves = jnp.where(slot_ids < sent_left[:, None], -1, jnp.where(slot_ids < (sent_left + kept_count)[:, None], 0, jnp.where(slot_ids < used_slots[:, None], 1, 0)))
    return (devices[:, None] + slot_moves).astype(jnp.int32)

def normalize_rows(values):
    widened = values.astype(jnp.float32)
    scale = lax.rsqrt(lax.optimization_barrier(jnp.mean(widened * widened, axis=-1, keepdims=True)) + epsilon)
    return (widened * scale).astype(jnp.bfloat16)

def settle(values):
    return lax.optimization_barrier(values.astype(jnp.bfloat16)).astype(jnp.float32)

def reference(hidden, queries, upstream, key_weight, value_weight, lengths, advantage):
    device_total = lengths.shape[0]
    slot_total = lengths.shape[1]
    group_size = QH // KVH
    inverse_root = HD ** (-0.5)
    offsets = jnp.arange(LMAX, dtype=jnp.int32)
    row_ids = jnp.arange(CAP_R, dtype=jnp.int32)
    learner = derive_learner(lengths)

    def one_device(carry, device):
        key_acc, value_acc = carry
        first_row = (device * CAP_R).astype(jnp.int32)
        hidden_rows = lax.dynamic_slice_in_dim(hidden, first_row, CAP_R, 0)
        query_rows = lax.dynamic_slice_in_dim(queries, first_row, CAP_R, 0)
        upstream_rows = lax.dynamic_slice_in_dim(upstream, first_row, CAP_R, 0)
        normed = normalize_rows(hidden_rows)
        key_rows = jnp.dot(normed, key_weight, preferred_element_type=jnp.float32).astype(jnp.bfloat16)
        value_rows = jnp.dot(normed, value_weight, preferred_element_type=jnp.float32).astype(jnp.bfloat16)
        slot_lengths = lengths[device].astype(jnp.int32)
        slot_ends = jnp.cumsum(slot_lengths).astype(jnp.int32)
        slot_starts = (slot_ends - slot_lengths).astype(jnp.int32)
        window = jnp.clip(slot_starts[:, None] + offsets[None, :], 0, CAP_R - 1).astype(jnp.int32)
        inside = offsets[None, :] < slot_lengths[:, None]
        rates = advantage[device] / jnp.maximum(slot_lengths, 1).astype(jnp.float32)
        normed_window = normed[window]
        query_window = query_rows[window].astype(jnp.float32).reshape(slot_total, LMAX, KVH, group_size, HD)
        key_window = key_rows[window].astype(jnp.float32).reshape(slot_total, LMAX, KVH, HD)
        value_window = value_rows[window].astype(jnp.float32).reshape(slot_total, LMAX, KVH, HD)
        cot_window = jnp.where(inside[:, :, None], rates[:, None, None] * upstream_rows[window].astype(jnp.float32), 0.0)
        cot_window = settle(cot_window).reshape(slot_total, LMAX, KVH, group_size, HD)
        allowed = (offsets[None, :] <= offsets[:, None])[None, :, :] & inside[:, None, :]
        scores = jnp.einsum('rtkgd,rukd->rkgtu', query_window, key_window) * inverse_root
        scores = jnp.where(allowed[:, None, None, :, :], scores, masked_score)
        row_peak = lax.optimization_barrier(jnp.max(scores, axis=-1, keepdims=True))
        raised = jnp.exp(scores - row_peak)
        probability = raised / lax.optimization_barrier(jnp.sum(raised, axis=-1, keepdims=True))
        weights = settle(probability)
        attended = jnp.einsum('rkgtu,rukd->rtkgd', weights, value_window).astype(jnp.bfloat16)
        prob_grad = jnp.einsum('rtkgd,rukd->rkgtu', cot_window, value_window)
        centre = lax.optimization_barrier(jnp.sum(probability * prob_grad, axis=-1, keepdims=True))
        score_grad = settle(probability * (prob_grad - centre))
        key_cot = (jnp.einsum('rkgtu,rtkgd->rukd', score_grad, query_window) * inverse_root).astype(jnp.bfloat16)
        value_cot = jnp.einsum('rkgtu,rtkgd->rukd', weights, cot_window).astype(jnp.bfloat16)
        flat_normed = normed_window.reshape(slot_total * LMAX, D)
        key_acc = key_acc + jnp.dot(flat_normed.T, key_cot.reshape(slot_total * LMAX, KVH * HD), preferred_element_type=jnp.float32)
        value_acc = value_acc + jnp.dot(flat_normed.T, value_cot.reshape(slot_total * LMAX, KVH * HD), preferred_element_type=jnp.float32)
        slot_of_row = jnp.minimum(lax.optimization_barrier(jnp.sum((row_ids[:, None] >= slot_ends[None, :]).astype(jnp.int32), axis=1)), slot_total - 1).astype(jnp.int32)
        offset_of_row = jnp.clip(row_ids - slot_starts[slot_of_row], 0, LMAX - 1).astype(jnp.int32)
        attended_rows = attended.reshape(slot_total * LMAX, QH * HD)[slot_of_row * LMAX + offset_of_row]
        return ((key_acc, value_acc), attended_rows)
    empty = jnp.zeros((D, KVH * HD), jnp.float32)
    (key_grad, value_grad), attended_all = lax.scan(one_device, (empty, empty), jnp.arange(device_total, dtype=jnp.int32))
    attended_flat = attended_all.reshape(device_total * CAP_R, QH * HD)
    flat_lengths = lengths.reshape(-1).astype(jnp.int32)
    flat_dest = learner.reshape(-1).astype(jnp.int32)
    dest_hits = (flat_dest[:, None] == jnp.arange(device_total, dtype=jnp.int32)[None, :]).astype(jnp.int32)
    lane_tokens = dest_hits * flat_lengths[:, None]
    before = (jnp.cumsum(lane_tokens, axis=0).astype(jnp.int32) - lane_tokens).astype(jnp.int32)
    learner_start = lax.optimization_barrier(jnp.sum(before * dest_hits, axis=1)).astype(jnp.int32)
    all_ends = jnp.cumsum(lengths.astype(jnp.int32), axis=1).astype(jnp.int32)
    device_base = (jnp.arange(device_total, dtype=jnp.int32) * CAP_R).astype(jnp.int32)
    rollout_start = (device_base[:, None] + all_ends - lengths.astype(jnp.int32)).reshape(-1).astype(jnp.int32)
    learner_rows = jnp.arange(device_total * CAP_L, dtype=jnp.int32)
    target = (learner_rows // CAP_L).astype(jnp.int32)
    within = (learner_rows % CAP_L).astype(jnp.int32)
    hits = (flat_dest[None, :] == target[:, None]) & (learner_start[None, :] <= within[:, None]) & (within[:, None] < learner_start[None, :] + flat_lengths[None, :])
    source = lax.optimization_barrier(jnp.sum(jnp.where(hits, rollout_start[None, :] + within[:, None] - learner_start[None, :], 0), axis=1)).astype(jnp.int32)
    filled = jnp.any(hits, axis=1)
    attention_out = jnp.where(filled[:, None], attended_flat[source], jnp.zeros((), jnp.bfloat16))
    return (attention_out, key_grad, value_grad)
```

```python
import functools

import jax
import jax.numpy as jnp
from jax import lax
from jax.experimental import pallas as pl
from jax.experimental.pallas import tpu as pltpu
from jax.sharding import PartitionSpec as P

HD = 128
BLOCK = 64
HALF = 2 * BLOCK
CAP_L = 4 * BLOCK
CHUNKS = 4

epsilon = 1e-06
masked_score = -1e30
mesh_id = pl.DeviceIdType.MESH
across = (((1,), (1,)), ((), ()))
down = (((0,), (0,)), ((), ()))


def dot32(a, b):
    return jnp.dot(a, b, preferred_element_type=jnp.float32)


def flag(condition):
    return jnp.where(condition, 1, 0).astype(jnp.int32)


def device_facts(lengths, d):
    slots = lengths.shape[1]
    used = jnp.int32(0)
    for r in range(slots):
        used += flag(lengths[d, r] > 0)
    heavy = flag(used >= 6)
    return used, heavy, heavy * ((used - 4) // 2)


def slot_length(lengths, d, slot, valid):
    return jnp.where(valid > 0, lengths[d, jnp.minimum(slot, lengths.shape[1] - 1)], 0)


def slot_start(lengths, d, slot):
    start = jnp.int32(0)
    for r in range(lengths.shape[1]):
        start += jnp.where(r < slot, lengths[d, r], 0)
    return start


def fused_kernel(count, lengths, advantage, hidden_hbm, query_hbm, upstream_hbm, key_hbm, value_hbm,
                 out_ref, key_grad_ref, value_grad_ref,
                 hidden_ref, query_ref, upstream_ref, weight_ref, pick_ref, place_ref,
                 piece_h, piece_qu, inc_h, inc_qu, full, qu, kv_acc, squares, out_buf, out_right_buf, out_in,
                 cots_ref, slices, acc,
                 local_done, piece_sent, piece_got, mp_sent, mp_got, s1_sent, s1_got, s2_sent, s2_got,
                 cot_sent, cot_got, out_sent, out_got):
    me, m = lax.axis_index("dp"), lax.axis_index("mp")
    half, core = m // 2, m % 2
    near, far = half * 2 + 1 - core, (1 - half) * 2 + core
    owners, _, width = full.shape
    chunk = width // CHUNKS
    heads = query_ref.shape[1] // HD
    share = slices.shape[4]
    per = width // share
    part = HALF // owners
    place = me % 4
    middle = (place == 1) | (place == 2)
    has_left, has_right = me > 0, me < count - 1

    fetches = [
        pltpu.make_async_copy(source, target, local_done.at[n])
        for n, (source, target) in enumerate((
            (hidden_hbm, hidden_ref),
            (query_hbm, query_ref),
            (upstream_hbm, upstream_ref),
            (key_hbm, weight_ref.at[:, :HD]),
            (value_hbm, weight_ref.at[:, HD:]),
        ))
    ]

    def piece_copy(side, p):
        if p < CHUNKS:
            columns = slice(p * chunk, (p + 1) * chunk)
            source, target = piece_h.at[side, :, columns], inc_h.at[:, columns]
        else:
            source, target = piece_qu.at[side], inc_qu
        return pltpu.make_async_remote_copy(
            src_ref=source, dst_ref=target, send_sem=piece_sent.at[side, p], recv_sem=piece_got.at[p],
            device_id={"dp": me + 2 * side - 1}, device_id_type=mesh_id,
        )

    def over_mp(h, kind, c):
        owner, target = ((m, near), (m, far), (far, near))[kind]
        spot = full.at[owner, h * HALF : (h + 1) * HALF, c * chunk : (c + 1) * chunk]
        return pltpu.make_async_remote_copy(
            src_ref=spot, dst_ref=spot, send_sem=mp_sent.at[h, kind, c], recv_sem=mp_got.at[h, kind, c],
            device_id={"mp": target}, device_id_type=mesh_id,
        )

    def slice_out(h, j):
        rows = pl.ds(pl.multiple_of(h * HALF + m * part, part), part)
        columns = pl.ds(pl.multiple_of(j % per * share, share), share)
        return pltpu.make_async_remote_copy(
            src_ref=full.at[j // per, rows, columns], dst_ref=slices.at[h, me, m],
            send_sem=s1_sent.at[h, j], recv_sem=s1_got.at[h, me],
            device_id={"dp": j}, device_id_type=mesh_id,
        )

    def slice_in(h, j):
        return pltpu.make_async_remote_copy(
            src_ref=slices.at[h, j, m], dst_ref=slices.at[h, j, m],
            send_sem=s1_sent.at[h, j], recv_sem=s1_got.at[h, j],
            device_id={"dp": j}, device_id_type=mesh_id,
        )

    def slices_mp(h, kind):
        owner, target = ((m, near), (m, far), (far, near))[kind]
        return pltpu.make_async_remote_copy(
            src_ref=slices.at[h, :, owner], dst_ref=slices.at[h, :, owner],
            send_sem=s2_sent.at[h, kind], recv_sem=s2_got.at[h, kind],
            device_id={"mp": target}, device_id_type=mesh_id,
        )

    def cots_of(h, d):
        return cots_ref.at[h, :, pl.ds(pl.multiple_of(d * HALF, HALF), HALF)]

    def cot_out(h, j):
        return pltpu.make_async_remote_copy(
            src_ref=cots_of(h, me), dst_ref=cots_of(h, me), send_sem=cot_sent.at[h, j], recv_sem=cot_got.at[h, me],
            device_id={"dp": j}, device_id_type=mesh_id,
        )

    def cot_in(h, j):
        return pltpu.make_async_remote_copy(
            src_ref=cots_of(h, j), dst_ref=cots_of(h, j), send_sem=cot_sent.at[h, j], recv_sem=cot_got.at[h, j],
            device_id={"dp": j}, device_id_type=mesh_id,
        )

    def out_copy(side):
        source, target = (out_buf.at[:BLOCK], out_in.at[BLOCK:]) if side == 0 else (out_right_buf, out_in.at[:BLOCK])
        return pltpu.make_async_remote_copy(
            src_ref=source, dst_ref=target, send_sem=out_sent.at[side], recv_sem=out_got.at[side],
            device_id={"dp": me + 2 * side - 1}, device_id_type=mesh_id,
        )

    gives_left = has_left & (place != 2)
    gives_right = has_right & (place != 1)
    takes_left = has_left & (place != 2)
    takes_right = has_right & (place != 1)

    def others(body):
        @pl.loop(1, count)
        def _(k):
            body(lax.rem(me + k, count))

    for fetch in fetches:
        fetch.start()
    barrier = pltpu.get_barrier_semaphore()
    for target in (near, far):
        pl.semaphore_signal(barrier, inc=1, device_id={"mp": target}, device_id_type=mesh_id)
    others(lambda j: pl.semaphore_signal(barrier, inc=1, device_id={"dp": j}, device_id_type=mesh_id))

    source = jnp.where(place <= 1, me + 1, me - 1)
    used, heavy, left_slots = device_facts(lengths, me)
    s_used, s_heavy, s_left = device_facts(lengths, source)
    kept = jnp.where(heavy > 0, 4, used)
    wanted = []
    for b in range(4):
        wanted.append((left_slots + b, flag(b < kept)))
    for b in range(2):
        wanted.append((jnp.int32(b), heavy * flag(b < left_slots)))
    for b in range(2):
        slot = left_slots + 4 + b
        wanted.append((slot, heavy * flag(slot < used)))
    sizes = [slot_length(lengths, me, slot, valid) for slot, valid in wanted]
    own_sizes = sizes[:4]
    own_rates = [advantage[me, jnp.minimum(slot, lengths.shape[1] - 1)] for slot, _ in wanted[:4]]
    in_sizes, in_rates = [], []
    for b in range(2):
        slot = jnp.where(place <= 1, b, s_left + 4 + b)
        valid = s_heavy * jnp.where(place <= 1, flag(b < s_left), flag(slot < s_used))
        in_sizes.append(slot_length(lengths, source, slot, valid))
        in_rates.append(advantage[source, jnp.minimum(slot, lengths.shape[1] - 1)])
    block_sizes = own_sizes[:2] + [own_sizes[2 + b] + in_sizes[b] for b in range(2)]
    block_rates = own_rates[:2] + [jnp.where(in_sizes[b] > 0, in_rates[b], own_rates[2 + b]) for b in range(2)]

    row_of = lax.broadcasted_iota(jnp.int32, (BLOCK, hidden_ref.shape[0]), 0)
    ahead = lax.broadcasted_iota(jnp.int32, (BLOCK, hidden_ref.shape[0]), 1) - row_of
    for b, (slot, _) in enumerate(wanted):
        hit = (ahead == slot_start(lengths, me, slot)) & (row_of < sizes[b])
        pick_ref[b * BLOCK : (b + 1) * BLOCK] = jnp.where(hit, 1.0, 0.0).astype(jnp.bfloat16)

    pl.semaphore_wait(barrier, count + 1)

    fetches[0].wait()
    for c in range(CHUNKS):
        columns = slice(c * chunk, (c + 1) * chunk)

        @pl.when(middle)
        def _():
            both = dot32(pick_ref[CAP_L:], hidden_ref[:, columns]).astype(jnp.bfloat16)
            for side in range(2):
                piece_h[side, :, columns] = both[side * HALF : (side + 1) * HALF]
                piece_copy(side, c).start()

        full[m, :HALF, columns] = dot32(pick_ref[:HALF], hidden_ref[:, columns]).astype(jnp.bfloat16)
        over_mp(0, 1, c).start()
        over_mp(0, 0, c).start()

    fetches[1].wait()
    fetches[2].wait()

    def spread(rows, store):
        for base, array in ((0, query_ref), (heads, upstream_ref)):
            for at in range(0, heads, 4):
                picked = dot32(pick_ref[rows], array[:, at * HD : (at + 4) * HD]).astype(jnp.bfloat16)
                for h in range(4):
                    store(base + at + h, picked[:, h * HD : (h + 1) * HD])

    @pl.when(middle)
    def _():
        def store(h, values):
            piece_qu[0, h] = values[:HALF]
            piece_qu[1, h] = values[HALF:]

        spread(slice(CAP_L, 2 * CAP_L), store)
        for side in range(2):
            piece_copy(side, CHUNKS).start()

    def store_own(h, values):
        qu[h] = values

    spread(slice(0, CAP_L), store_own)
    fetches[3].wait()
    fetches[4].wait()

    def absorb(h, c):
        total = jnp.zeros(kv_acc.shape, jnp.float32) if c == 0 else kv_acc[...]
        squared = jnp.zeros(squares.shape, jnp.float32) if c == 0 else squares[...]
        for owner in range(owners):
            block = full[owner, h * HALF : (h + 1) * HALF, c * chunk : (c + 1) * chunk]
            spot = owner * width + c * chunk
            total += dot32(block, weight_ref[spot : spot + chunk])
            for at in range(0, chunk, HD):
                wide = block[:, at : at + HD].astype(jnp.float32)
                squared += wide * wide
        kv_acc[...] = total
        squares[...] = squared

    def arrived(h, c):
        over_mp(h, 0, c).wait_recv()
        over_mp(h, 2, c).wait_recv()
        absorb(h, c)

    for c in range(CHUNKS):
        columns = slice(c * chunk, (c + 1) * chunk)
        over_mp(0, 1, c).wait_recv()
        over_mp(0, 2, c).start()
        own = dot32(pick_ref[HALF:CAP_L], hidden_ref[:, columns])
        piece_copy(0, c).wait_recv()
        full[m, HALF:, columns] = (own + inc_h[:, columns].astype(jnp.float32)).astype(jnp.bfloat16)
        over_mp(1, 1, c).start()
        over_mp(1, 0, c).start()
        if c > 0:
            arrived(0, c - 1)
    arrived(0, CHUNKS - 1)

    def local_slice(h):
        columns = pl.ds(pl.multiple_of(me % per * share, share), share)
        rows = pl.ds(pl.multiple_of(h * HALF + m * part, part), part)
        slices[h, me, m] = full[me // per, rows, columns]

    def attend(h):
        scale = lax.rsqrt(jnp.sum(squares[...], axis=1, keepdims=True) / (owners * width) + epsilon)
        keys_values = (kv_acc[...] * scale).astype(jnp.bfloat16)
        inverse_root = HD ** (-0.5)
        u = lax.broadcasted_iota(jnp.int32, (BLOCK, heads * BLOCK), 0)
        t = lax.broadcasted_iota(jnp.int32, (BLOCK, heads * BLOCK), 1) % BLOCK
        allowed = u <= t
        row = lax.broadcasted_iota(jnp.int32, (BLOCK, HD), 0)
        terms = []
        for b in range(2):
            block = 2 * h + b
            rows = slice(block * BLOCK, (block + 1) * BLOCK)
            key, value = (keys_values[b * BLOCK : (b + 1) * BLOCK, at : at + HD] for at in (0, HD))
            size = jnp.full((BLOCK, HD), block_sizes[block], jnp.int32)
            rate = jnp.full((BLOCK, HD), block_rates[block], jnp.float32) / jnp.maximum(size, 1).astype(jnp.float32)
            rate = jnp.where(row < size, rate, 0.0)
            query = qu[:heads, rows].reshape(heads * BLOCK, HD)
            cot = (qu[heads:, rows].astype(jnp.float32) * rate[None]).astype(jnp.bfloat16).reshape(heads * BLOCK, HD)
            scores = lax.dot_general(key, query, across, preferred_element_type=jnp.float32) * inverse_root
            scores = jnp.where(allowed, scores, masked_score)
            raised = jnp.exp(scores - jnp.max(scores, axis=0, keepdims=True))
            probability = raised * (1.0 / jnp.sum(raised, axis=0, keepdims=True))
            weights = probability.astype(jnp.bfloat16)
            attended = lax.dot_general(weights, value, down, preferred_element_type=jnp.float32).astype(jnp.bfloat16)
            for q in range(heads):
                out_buf[rows, q * HD : (q + 1) * HD] = attended[q * BLOCK : (q + 1) * BLOCK]
            prob_grad = lax.dot_general(value, cot, across, preferred_element_type=jnp.float32)
            centre = jnp.sum(probability * prob_grad, axis=0, keepdims=True)
            score_grad = (probability * (prob_grad - centre)).astype(jnp.bfloat16)
            key_cot = dot32(score_grad, query) * inverse_root
            value_cot = dot32(weights, cot)
            terms.append(jnp.concatenate([key_cot, value_cot], axis=1))
        cots = jnp.concatenate(terms, axis=0) * scale
        cots_ref[h, :, pl.ds(pl.multiple_of(me * HALF, HALF), HALF)] = cots.T.astype(jnp.bfloat16)

    others(lambda j: slice_out(0, j).start())
    local_slice(0)
    attend(0)
    others(lambda j: cot_out(0, j).start())

    @pl.when(gives_left)
    def _():
        out_copy(0).start()

    for c in range(CHUNKS):
        over_mp(1, 1, c).wait_recv()
        over_mp(1, 2, c).start()
        if c > 0:
            arrived(1, c - 1)
    arrived(1, CHUNKS - 1)
    others(lambda j: slice_out(1, j).start())
    local_slice(1)
    piece_copy(0, CHUNKS).wait_recv()
    for h in range(2 * heads):
        qu[h, HALF:] = (qu[h, HALF:].astype(jnp.float32) + inc_qu[h].astype(jnp.float32)).astype(jnp.bfloat16)
    attend(1)
    others(lambda j: cot_out(1, j).start())

    no_left = flag(has_left) * (1 - device_facts(lengths, jnp.maximum(me - 1, 0))[1])
    sends_two = jnp.full((BLOCK, out_buf.shape[1]), no_left, jnp.int32) > 0
    out_right_buf[...] = jnp.where(
        sends_two, out_buf[HALF : HALF + BLOCK].astype(jnp.float32), out_buf[BLOCK:HALF].astype(jnp.float32)
    ).astype(jnp.bfloat16)

    @pl.when(gives_right)
    def _():
        out_copy(1).start()

    @pl.when(jnp.logical_not(takes_left))
    def _():
        out_in[:BLOCK] = jnp.zeros((BLOCK, out_in.shape[1]), jnp.bfloat16)

    @pl.when(jnp.logical_not(takes_right))
    def _():
        out_in[BLOCK:] = jnp.zeros((BLOCK, out_in.shape[1]), jnp.bfloat16)

    for h in range(2):
        others(lambda j: slice_in(h, j).wait_recv())
        slices_mp(h, 1).start()
        slices_mp(h, 0).start()

    heavy_left = flag(has_left) * device_facts(lengths, jnp.maximum(me - 1, 0))[1]
    heavy_right = flag(has_right) * device_facts(lengths, jnp.minimum(me + 1, count - 1))[1]
    light = 1 - heavy
    gives = flag(has_left) * (1 - heavy_left)
    second = flag(me > 1) * (1 - device_facts(lengths, jnp.maximum(me - 2, 0))[1])
    from_left = light * flag(has_left) * (1 - heavy_left) * lengths[jnp.maximum(me - 1, 0), second + 1]
    from_right = light * flag(has_right) * (1 - heavy_right) * lengths[jnp.minimum(me + 1, count - 1), 0]
    total_in = in_sizes[0] + in_sizes[1]
    kept_size = lengths[me, gives]
    base_kept = from_left + heavy_left * total_in
    base_in = jnp.where(heavy_left > 0, 0, base_kept + kept_size)
    base_right = base_kept + kept_size + heavy_right * total_in
    spots = []
    running = jnp.int32(0)
    for b in range(4):
        if b < 2:
            size, at = jnp.where(gives == b, kept_size, 0), base_kept
        else:
            size, at = in_sizes[b - 2], base_in + (in_sizes[0] if b == 3 else 0)
        spots.append((jnp.where(heavy > 0, running, at), jnp.where(heavy > 0, own_sizes[b], size)))
        running = running + own_sizes[b]
    spots += [(jnp.int32(0), from_left), (base_right, from_right)]
    target = lax.broadcasted_iota(jnp.int32, (CAP_L, HALF), 0)
    lane = lax.broadcasted_iota(jnp.int32, (CAP_L, HALF), 1)
    first = lane < BLOCK
    offset = lane % BLOCK
    for pair in range(3):
        (at0, size0), (at1, size1) = spots[2 * pair : 2 * pair + 2]
        at = jnp.where(first, at0, at1)
        size = jnp.where(first, size0, size1)
        hit = (target - at == offset) & (offset < size)
        place_ref[:, pair * HALF : (pair + 1) * HALF] = jnp.where(hit, 1.0, 0.0).astype(jnp.bfloat16)

    @pl.when(takes_left)
    def _():
        out_copy(1).wait_recv()

    @pl.when(takes_right)
    def _():
        out_copy(0).wait_recv()

    for at in range(0, out_ref.shape[1], 256):
        columns = slice(at, at + 256)
        total = dot32(place_ref[:, :CAP_L], out_buf[:, columns]) + dot32(place_ref[:, CAP_L:], out_in[:, columns])
        out_ref[:, columns] = total.astype(jnp.bfloat16)

    for h in range(2):
        slices_mp(h, 1).wait_recv()
        slices_mp(h, 2).start()
    for h in range(2):
        others(lambda j: cot_in(h, j).wait_recv())
        slices_mp(h, 0).wait_recv()
        slices_mp(h, 2).wait_recv()
        tile = min(256, share)
        for at in range(0, share, tile):
            columns = slice(at, at + tile)
            rows = slices[h, :, :, :, columns].reshape(count * HALF, tile)
            term = dot32(cots_ref[h], rows)
            if h == 0:
                acc[:, columns] = term
            else:
                acc[:, columns] += term
    key_grad_ref[...] = acc[:HD].T
    value_grad_ref[...] = acc[HD:].T

    @pl.when(middle)
    def _():
        for side in range(2):
            for p in range(CHUNKS + 1):
                piece_copy(side, p).wait_send()

    @pl.when(gives_left)
    def _():
        out_copy(0).wait_send()

    @pl.when(gives_right)
    def _():
        out_copy(1).wait_send()

    for h in range(2):
        for kind in range(3):
            slices_mp(h, kind).wait_send()
            for c in range(CHUNKS):
                over_mp(h, kind, c).wait_send()

        def left(j):
            slice_out(h, j).wait_send()
            cot_out(h, j).wait_send()

        others(left)


def body(hidden, queries, upstream, key_weight, value_weight, lengths, advantage):
    count, owners = lax.axis_size("dp"), lax.axis_size("mp")
    rows, width = hidden.shape
    head_width = queries.shape[1]
    heads = head_width // HD
    depth = key_weight.shape[0]
    share = depth // count
    vmem = pl.BlockSpec(memory_space=pltpu.VMEM)
    smem = pl.BlockSpec(memory_space=pltpu.SMEM)
    bf16 = lambda *shape: pltpu.VMEM(shape, jnp.bfloat16)
    f32 = lambda *shape: pltpu.VMEM(shape, jnp.float32)
    sems = lambda *shape: pltpu.SemaphoreType.DMA(shape)
    return pl.pallas_call(
        functools.partial(fused_kernel, count),
        in_specs=[smem] * 2 + [pl.BlockSpec(memory_space=pl.ANY)] * 5,
        out_specs=[vmem] * 3,
        out_shape=[
            jax.ShapeDtypeStruct((CAP_L, head_width), jnp.bfloat16),
            jax.ShapeDtypeStruct((share, HD), jnp.float32),
            jax.ShapeDtypeStruct((share, HD), jnp.float32),
        ],
        scratch_shapes=[
            bf16(rows, width), bf16(rows, head_width), bf16(rows, head_width), bf16(depth, 2 * HD),
            bf16(8 * BLOCK, rows), bf16(CAP_L, CAP_L + HALF),
            bf16(2, HALF, width), bf16(2, 2 * heads, HALF, HD), bf16(HALF, width), bf16(2 * heads, HALF, HD),
            bf16(owners, CAP_L, width), bf16(2 * heads, CAP_L, HD), f32(HALF, 2 * HD), f32(HALF, HD),
            bf16(CAP_L, head_width), bf16(BLOCK, head_width), bf16(HALF, head_width),
            bf16(2, 2 * HD, count * HALF), bf16(2, count, owners, HALF // owners, share), f32(2 * HD, share),
            sems(5), sems(2, CHUNKS + 1), sems(CHUNKS + 1), sems(2, 3, CHUNKS), sems(2, 3, CHUNKS),
            sems(2, count), sems(2, count), sems(2, 3), sems(2, 3),
            sems(2, count), sems(2, count), sems(2), sems(2),
        ],
        compiler_params=pltpu.CompilerParams(
            collective_id=0, has_side_effects=True, vmem_limit_bytes=56 * 1024 * 1024
        ),
    )(lengths, advantage, hidden, queries, upstream, key_weight, value_weight)


def solution(mesh):
    in_specs = (P("dp", "mp"), P("dp", "mp"), P("dp", "mp"), P(None, "mp"), P(None, "mp"), P(), P())
    out_specs = (P("dp", "mp"), P("dp", "mp"), P("dp", "mp"))
    return jax.shard_map(body, mesh=mesh, in_specs=in_specs, out_specs=out_specs, check_vma=False)
```

```python
import functools

import jax
import jax.numpy as jnp
from jax import lax
from jax.experimental import pallas as pl
from jax.experimental.pallas import tpu as pltpu
from jax.sharding import PartitionSpec as P

HD = 128
BLOCK = 64
HALF = 2 * BLOCK
CAP_L = 4 * BLOCK
CHUNKS = 4

epsilon = 1e-06
masked_score = -1e30
mesh_id = pl.DeviceIdType.MESH
across = (((1,), (1,)), ((), ()))
down = (((0,), (0,)), ((), ()))


def dot32(a, b):
    return jnp.dot(a, b, preferred_element_type=jnp.float32)


def flag(condition):
    return jnp.where(condition, 1, 0).astype(jnp.int32)


def device_facts(lengths, d):
    slots = lengths.shape[1]
    used = jnp.int32(0)
    for r in range(slots):
        used += flag(lengths[d, r] > 0)
    heavy = flag(used >= 6)
    return used, heavy, heavy * ((used - 4) // 2)


def slot_length(lengths, d, slot, valid):
    return jnp.where(valid > 0, lengths[d, jnp.minimum(slot, lengths.shape[1] - 1)], 0)


def slot_start(lengths, d, slot):
    start = jnp.int32(0)
    for r in range(lengths.shape[1]):
        start += jnp.where(r < slot, lengths[d, r], 0)
    return start


def fused_kernel(count, lengths, advantage, hidden_hbm, query_hbm, upstream_hbm, key_hbm, value_hbm,
                 out_ref, key_grad_ref, value_grad_ref,
                 hidden_ref, query_ref, upstream_ref, weight_ref, pick_ref, place_ref,
                 piece_h, piece_qu, inc_h, inc_qu, full, qu, kv_acc, squares, out_buf, out_right_buf, out_in,
                 cots_ref, slices, acc,
                 local_done, piece_sent, piece_got, mp_sent, mp_got, s1_sent, s1_got, s2_sent, s2_got,
                 cot_sent, cot_passed, cot_got, out_sent, out_got):
    me, m = lax.axis_index("dp"), lax.axis_index("mp")
    half, core = m // 2, m % 2
    near, far = half * 2 + 1 - core, (1 - half) * 2 + core
    owners, _, width = full.shape
    chunk = width // CHUNKS
    heads = query_ref.shape[1] // HD
    share = slices.shape[4]
    per = width // share
    part = HALF // owners
    place = me % 4
    middle = (place == 1) | (place == 2)
    has_left, has_right = me > 0, me < count - 1
    line, side_y, lines = me // 2, me % 2, count // 2
    partner = line * 2 + 1 - side_y

    fetches = [
        pltpu.make_async_copy(source, target, local_done.at[n])
        for n, (source, target) in enumerate((
            (hidden_hbm, hidden_ref),
            (query_hbm, query_ref),
            (upstream_hbm, upstream_ref),
            (key_hbm, weight_ref.at[:, :HD]),
            (value_hbm, weight_ref.at[:, HD:]),
        ))
    ]

    def piece_copy(side, p):
        if p < CHUNKS:
            columns = slice(p * chunk, (p + 1) * chunk)
            source, target = piece_h.at[side, :, columns], inc_h.at[:, columns]
        else:
            source, target = piece_qu.at[side], inc_qu
        return pltpu.make_async_remote_copy(
            src_ref=source, dst_ref=target, send_sem=piece_sent.at[side, p], recv_sem=piece_got.at[p],
            device_id={"dp": me + 2 * side - 1}, device_id_type=mesh_id,
        )

    def over_mp(h, kind, c):
        owner, target = ((m, near), (m, far), (far, near))[kind]
        spot = full.at[owner, h * HALF : (h + 1) * HALF, c * chunk : (c + 1) * chunk]
        return pltpu.make_async_remote_copy(
            src_ref=spot, dst_ref=spot, send_sem=mp_sent.at[h, kind, c], recv_sem=mp_got.at[h, kind, c],
            device_id={"mp": target}, device_id_type=mesh_id,
        )

    def slice_out(h, j):
        rows = pl.ds(pl.multiple_of(h * HALF + m * part, part), part)
        columns = pl.ds(pl.multiple_of(j % per * share, share), share)
        return pltpu.make_async_remote_copy(
            src_ref=full.at[j // per, rows, columns], dst_ref=slices.at[h, me, m],
            send_sem=s1_sent.at[h, j], recv_sem=s1_got.at[h, me],
            device_id={"dp": j}, device_id_type=mesh_id,
        )

    def slice_in(h, j):
        return pltpu.make_async_remote_copy(
            src_ref=slices.at[h, j, m], dst_ref=slices.at[h, j, m],
            send_sem=s1_sent.at[h, j], recv_sem=s1_got.at[h, j],
            device_id={"dp": j}, device_id_type=mesh_id,
        )

    def slices_mp(h, kind, i):
        owner, target = ((m, near), (m, far), (far, near))[kind]
        spot = slices.at[h, i, owner]
        return pltpu.make_async_remote_copy(
            src_ref=spot, dst_ref=spot, send_sem=s2_sent.at[h, kind, i], recv_sem=s2_got.at[h, kind, i],
            device_id={"mp": target}, device_id_type=mesh_id,
        )

    def cots_of(h, d):
        return cots_ref.at[h, :, pl.ds(pl.multiple_of(d * HALF, HALF), HALF)]

    def cot_out(h, j):
        return pltpu.make_async_remote_copy(
            src_ref=cots_of(h, me), dst_ref=cots_of(h, me), send_sem=cot_sent.at[h, j], recv_sem=cot_got.at[h, me],
            device_id={"dp": j}, device_id_type=mesh_id,
        )

    def cot_on(h, j):
        return pltpu.make_async_remote_copy(
            src_ref=cots_of(h, j), dst_ref=cots_of(h, j), send_sem=cot_passed.at[h, j], recv_sem=cot_got.at[h, j],
            device_id={"dp": partner}, device_id_type=mesh_id,
        )

    def out_copy(side):
        source, target = (out_buf.at[:BLOCK], out_in.at[BLOCK:]) if side == 0 else (out_right_buf, out_in.at[:BLOCK])
        return pltpu.make_async_remote_copy(
            src_ref=source, dst_ref=target, send_sem=out_sent.at[side], recv_sem=out_got.at[side],
            device_id={"dp": me + 2 * side - 1}, device_id_type=mesh_id,
        )

    gives_left = has_left & (place != 2)
    gives_right = has_right & (place != 1)
    takes_left = has_left & (place != 2)
    takes_right = has_right & (place != 1)

    def others(body):
        @pl.loop(1, count)
        def _(k):
            body(lax.rem(me + k, count))

    def along_line(body):
        @pl.loop(1, lines)
        def _(k):
            body(lax.rem(line + k, lines) * 2 + side_y)

    def send_slices(h, block, first, last):
        @pl.loop(first, last)
        def _(e):
            j = block * per + e

            @pl.when(j != me)
            def _():
                slice_out(h, j).start()

    def finished(c):
        return max(c * chunk // share, 0), (c + 1) * chunk // share

    def send_cots(h):
        along_line(lambda j: cot_out(h, j).start())
        cot_out(h, partner).start()

    def pass_cots(h):
        def one(j):
            cot_on(h, j).wait_recv()
            cot_on(h, j).start()

        along_line(one)

    def send_over_mp(h):
        def one(i):
            slice_in(h, i).wait_recv()
            slices_mp(h, 1, i).start()
            slices_mp(h, 0, i).start()

        others(one)

    def relay_over_mp(h):
        def one(i):
            slices_mp(h, 1, i).wait_recv()
            slices_mp(h, 2, i).start()

        others(one)

    for fetch in fetches:
        fetch.start()
    barrier = pltpu.get_barrier_semaphore()
    for target in (near, far):
        pl.semaphore_signal(barrier, inc=1, device_id={"mp": target}, device_id_type=mesh_id)
    others(lambda j: pl.semaphore_signal(barrier, inc=1, device_id={"dp": j}, device_id_type=mesh_id))

    source = jnp.where(place <= 1, me + 1, me - 1)
    used, heavy, left_slots = device_facts(lengths, me)
    s_used, s_heavy, s_left = device_facts(lengths, source)
    kept = jnp.where(heavy > 0, 4, used)
    wanted = []
    for b in range(4):
        wanted.append((left_slots + b, flag(b < kept)))
    for b in range(2):
        wanted.append((jnp.int32(b), heavy * flag(b < left_slots)))
    for b in range(2):
        slot = left_slots + 4 + b
        wanted.append((slot, heavy * flag(slot < used)))
    sizes = [slot_length(lengths, me, slot, valid) for slot, valid in wanted]
    own_sizes = sizes[:4]
    own_rates = [advantage[me, jnp.minimum(slot, lengths.shape[1] - 1)] for slot, _ in wanted[:4]]
    in_sizes, in_rates = [], []
    for b in range(2):
        slot = jnp.where(place <= 1, b, s_left + 4 + b)
        valid = s_heavy * jnp.where(place <= 1, flag(b < s_left), flag(slot < s_used))
        in_sizes.append(slot_length(lengths, source, slot, valid))
        in_rates.append(advantage[source, jnp.minimum(slot, lengths.shape[1] - 1)])
    block_sizes = own_sizes[:2] + [own_sizes[2 + b] + in_sizes[b] for b in range(2)]
    block_rates = own_rates[:2] + [jnp.where(in_sizes[b] > 0, in_rates[b], own_rates[2 + b]) for b in range(2)]

    row_of = lax.broadcasted_iota(jnp.int32, (BLOCK, hidden_ref.shape[0]), 0)
    ahead = lax.broadcasted_iota(jnp.int32, (BLOCK, hidden_ref.shape[0]), 1) - row_of
    for b, (slot, _) in enumerate(wanted):
        hit = (ahead == slot_start(lengths, me, slot)) & (row_of < sizes[b])
        pick_ref[b * BLOCK : (b + 1) * BLOCK] = jnp.where(hit, 1.0, 0.0).astype(jnp.bfloat16)

    pl.semaphore_wait(barrier, count + 1)

    fetches[0].wait()
    for c in range(CHUNKS):
        columns = slice(c * chunk, (c + 1) * chunk)

        @pl.when(middle)
        def _():
            both = dot32(pick_ref[CAP_L:], hidden_ref[:, columns]).astype(jnp.bfloat16)
            for side in range(2):
                piece_h[side, :, columns] = both[side * HALF : (side + 1) * HALF]
                piece_copy(side, c).start()

        full[m, :HALF, columns] = dot32(pick_ref[:HALF], hidden_ref[:, columns]).astype(jnp.bfloat16)
        over_mp(0, 1, c).start()
        over_mp(0, 0, c).start()

    send_slices(0, m, 0, per)
    for c in range(CHUNKS):
        over_mp(0, 0, c).wait_recv()
    send_slices(0, near, 0, per)
    fetches[1].wait()
    fetches[2].wait()

    def spread(rows, store):
        for base, array in ((0, query_ref), (heads, upstream_ref)):
            for at in range(0, heads, 4):
                picked = dot32(pick_ref[rows], array[:, at * HD : (at + 4) * HD]).astype(jnp.bfloat16)
                for h in range(4):
                    store(base + at + h, picked[:, h * HD : (h + 1) * HD])

    @pl.when(middle)
    def _():
        def store(h, values):
            piece_qu[0, h] = values[:HALF]
            piece_qu[1, h] = values[HALF:]

        spread(slice(CAP_L, 2 * CAP_L), store)
        for side in range(2):
            piece_copy(side, CHUNKS).start()

    def store_own(h, values):
        qu[h] = values

    spread(slice(0, CAP_L), store_own)
    fetches[3].wait()
    fetches[4].wait()

    def absorb(h, c):
        total = jnp.zeros(kv_acc.shape, jnp.float32) if c == 0 else kv_acc[...]
        squared = jnp.zeros(squares.shape, jnp.float32) if c == 0 else squares[...]
        for owner in range(owners):
            block = full[owner, h * HALF : (h + 1) * HALF, c * chunk : (c + 1) * chunk]
            spot = owner * width + c * chunk
            total += dot32(block, weight_ref[spot : spot + chunk])
            for at in range(0, chunk, HD):
                wide = block[:, at : at + HD].astype(jnp.float32)
                squared += wide * wide
        kv_acc[...] = total
        squares[...] = squared

    corner = (1 - half) * 2 + 1 - core

    def arrived(h, c):
        over_mp(h, 2, c).wait_recv()
        first, last = finished(c)
        if last > first:
            for block in (far, corner):
                send_slices(h, block, first, last)
        absorb(h, c)

    for c in range(CHUNKS):
        columns = slice(c * chunk, (c + 1) * chunk)
        over_mp(0, 1, c).wait_recv()
        over_mp(0, 2, c).start()
        own = dot32(pick_ref[HALF:CAP_L], hidden_ref[:, columns])
        piece_copy(0, c).wait_recv()
        full[m, HALF:, columns] = (own + inc_h[:, columns].astype(jnp.float32)).astype(jnp.bfloat16)
        over_mp(1, 1, c).start()
        over_mp(1, 0, c).start()
        if c > 0:
            arrived(0, c - 1)
    arrived(0, CHUNKS - 1)

    def local_slice(h):
        columns = pl.ds(pl.multiple_of(me % per * share, share), share)
        slices[h, me] = full[me // per, h * HALF : (h + 1) * HALF, columns].reshape(owners, part, share)

    def attend(h):
        scale = lax.rsqrt(jnp.sum(squares[...], axis=1, keepdims=True) / (owners * width) + epsilon)
        keys_values = (kv_acc[...] * scale).astype(jnp.bfloat16)
        inverse_root = HD ** (-0.5)
        u = lax.broadcasted_iota(jnp.int32, (BLOCK, heads * BLOCK), 0)
        t = lax.broadcasted_iota(jnp.int32, (BLOCK, heads * BLOCK), 1) % BLOCK
        allowed = u <= t
        row = lax.broadcasted_iota(jnp.int32, (BLOCK, HD), 0)
        terms = []
        for b in range(2):
            block = 2 * h + b
            rows = slice(block * BLOCK, (block + 1) * BLOCK)
            key, value = (keys_values[b * BLOCK : (b + 1) * BLOCK, at : at + HD] for at in (0, HD))
            size = jnp.full((BLOCK, HD), block_sizes[block], jnp.int32)
            rate = jnp.full((BLOCK, HD), block_rates[block], jnp.float32) / jnp.maximum(size, 1).astype(jnp.float32)
            rate = jnp.where(row < size, rate, 0.0)
            query = qu[:heads, rows].reshape(heads * BLOCK, HD)
            cot = (qu[heads:, rows].astype(jnp.float32) * rate[None]).astype(jnp.bfloat16).reshape(heads * BLOCK, HD)
            scores = lax.dot_general(key, query, across, preferred_element_type=jnp.float32) * inverse_root
            scores = jnp.where(allowed, scores, masked_score)
            raised = jnp.exp(scores - jnp.max(scores, axis=0, keepdims=True))
            probability = raised * (1.0 / jnp.sum(raised, axis=0, keepdims=True))
            weights = probability.astype(jnp.bfloat16)
            attended = lax.dot_general(weights, value, down, preferred_element_type=jnp.float32).astype(jnp.bfloat16)
            for q in range(heads):
                out_buf[rows, q * HD : (q + 1) * HD] = attended[q * BLOCK : (q + 1) * BLOCK]
            prob_grad = lax.dot_general(value, cot, across, preferred_element_type=jnp.float32)
            centre = jnp.sum(probability * prob_grad, axis=0, keepdims=True)
            score_grad = (probability * (prob_grad - centre)).astype(jnp.bfloat16)
            key_cot = dot32(score_grad, query) * inverse_root
            value_cot = dot32(weights, cot)
            terms.append(jnp.concatenate([key_cot, value_cot], axis=1))
        cots = jnp.concatenate(terms, axis=0) * scale
        cots_ref[h, :, pl.ds(pl.multiple_of(me * HALF, HALF), HALF)] = cots.T.astype(jnp.bfloat16)

    attend(0)
    send_cots(0)
    send_slices(1, m, 0, per)
    for c in range(CHUNKS):
        over_mp(1, 0, c).wait_recv()
    send_slices(1, near, 0, per)
    local_slice(0)

    @pl.when(gives_left)
    def _():
        out_copy(0).start()

    for c in range(CHUNKS):
        over_mp(1, 1, c).wait_recv()
        over_mp(1, 2, c).start()
        if c > 0:
            arrived(1, c - 1)
        if c == CHUNKS // 2:
            pass_cots(0)
    send_over_mp(0)
    arrived(1, CHUNKS - 1)
    piece_copy(0, CHUNKS).wait_recv()
    for h in range(2 * heads):
        qu[h, HALF:] = (qu[h, HALF:].astype(jnp.float32) + inc_qu[h].astype(jnp.float32)).astype(jnp.bfloat16)
    attend(1)
    send_cots(1)
    local_slice(1)

    no_left = flag(has_left) * (1 - device_facts(lengths, jnp.maximum(me - 1, 0))[1])
    sends_two = jnp.full((BLOCK, out_buf.shape[1]), no_left, jnp.int32) > 0
    out_right_buf[...] = jnp.where(
        sends_two, out_buf[HALF : HALF + BLOCK].astype(jnp.float32), out_buf[BLOCK:HALF].astype(jnp.float32)
    ).astype(jnp.bfloat16)

    @pl.when(gives_right)
    def _():
        out_copy(1).start()

    @pl.when(jnp.logical_not(takes_left))
    def _():
        out_in[:BLOCK] = jnp.zeros((BLOCK, out_in.shape[1]), jnp.bfloat16)

    @pl.when(jnp.logical_not(takes_right))
    def _():
        out_in[BLOCK:] = jnp.zeros((BLOCK, out_in.shape[1]), jnp.bfloat16)

    relay_over_mp(0)
    send_over_mp(1)
    pass_cots(1)

    heavy_left = flag(has_left) * device_facts(lengths, jnp.maximum(me - 1, 0))[1]
    heavy_right = flag(has_right) * device_facts(lengths, jnp.minimum(me + 1, count - 1))[1]
    light = 1 - heavy
    gives = flag(has_left) * (1 - heavy_left)
    second = flag(me > 1) * (1 - device_facts(lengths, jnp.maximum(me - 2, 0))[1])
    from_left = light * flag(has_left) * (1 - heavy_left) * lengths[jnp.maximum(me - 1, 0), second + 1]
    from_right = light * flag(has_right) * (1 - heavy_right) * lengths[jnp.minimum(me + 1, count - 1), 0]
    total_in = in_sizes[0] + in_sizes[1]
    kept_size = lengths[me, gives]
    base_kept = from_left + heavy_left * total_in
    base_in = jnp.where(heavy_left > 0, 0, base_kept + kept_size)
    base_right = base_kept + kept_size + heavy_right * total_in
    spots = []
    running = jnp.int32(0)
    for b in range(4):
        if b < 2:
            size, at = jnp.where(gives == b, kept_size, 0), base_kept
        else:
            size, at = in_sizes[b - 2], base_in + (in_sizes[0] if b == 3 else 0)
        spots.append((jnp.where(heavy > 0, running, at), jnp.where(heavy > 0, own_sizes[b], size)))
        running = running + own_sizes[b]
    spots += [(jnp.int32(0), from_left), (base_right, from_right)]
    target = lax.broadcasted_iota(jnp.int32, (CAP_L, HALF), 0)
    lane = lax.broadcasted_iota(jnp.int32, (CAP_L, HALF), 1)
    first = lane < BLOCK
    offset = lane % BLOCK
    for pair in range(3):
        (at0, size0), (at1, size1) = spots[2 * pair : 2 * pair + 2]
        at = jnp.where(first, at0, at1)
        size = jnp.where(first, size0, size1)
        hit = (target - at == offset) & (offset < size)
        place_ref[:, pair * HALF : (pair + 1) * HALF] = jnp.where(hit, 1.0, 0.0).astype(jnp.bfloat16)

    @pl.when(takes_left)
    def _():
        out_copy(1).wait_recv()

    @pl.when(takes_right)
    def _():
        out_copy(0).wait_recv()

    for at in range(0, out_ref.shape[1], 256):
        columns = slice(at, at + 256)
        total = dot32(place_ref[:, :CAP_L], out_buf[:, columns]) + dot32(place_ref[:, CAP_L:], out_in[:, columns])
        out_ref[:, columns] = total.astype(jnp.bfloat16)

    relay_over_mp(1)
    for h in range(2):
        def gathered(i):
            slices_mp(h, 0, i).wait_recv()
            slices_mp(h, 2, i).wait_recv()

        others(gathered)
        cot_on(h, partner).wait_recv()
        along_line(lambda j: cot_on(h, j // 2 * 2 + 1 - side_y).wait_recv())
        tile = min(256, share)
        for at in range(0, share, tile):
            columns = slice(at, at + tile)
            rows = slices[h, :, :, :, columns].reshape(count * HALF, tile)
            term = dot32(cots_ref[h], rows)
            if h == 0:
                acc[:, columns] = term
            else:
                acc[:, columns] += term
    key_grad_ref[...] = acc[:HD].T
    value_grad_ref[...] = acc[HD:].T

    @pl.when(middle)
    def _():
        for side in range(2):
            for p in range(CHUNKS + 1):
                piece_copy(side, p).wait_send()

    @pl.when(gives_left)
    def _():
        out_copy(0).wait_send()

    @pl.when(gives_right)
    def _():
        out_copy(1).wait_send()

    for h in range(2):
        for kind in range(3):
            for c in range(CHUNKS):
                over_mp(h, kind, c).wait_send()

        def left(j):
            slice_out(h, j).wait_send()
            for kind in range(3):
                slices_mp(h, kind, j).wait_send()

        def passed(j):
            cot_out(h, j).wait_send()
            cot_on(h, j).wait_send()

        others(left)
        along_line(passed)
        cot_out(h, partner).wait_send()


def body(hidden, queries, upstream, key_weight, value_weight, lengths, advantage):
    count, owners = lax.axis_size("dp"), lax.axis_size("mp")
    rows, width = hidden.shape
    head_width = queries.shape[1]
    heads = head_width // HD
    depth = key_weight.shape[0]
    share = depth // count
    vmem = pl.BlockSpec(memory_space=pltpu.VMEM)
    smem = pl.BlockSpec(memory_space=pltpu.SMEM)
    bf16 = lambda *shape: pltpu.VMEM(shape, jnp.bfloat16)
    f32 = lambda *shape: pltpu.VMEM(shape, jnp.float32)
    sems = lambda *shape: pltpu.SemaphoreType.DMA(shape)
    return pl.pallas_call(
        functools.partial(fused_kernel, count),
        in_specs=[smem] * 2 + [pl.BlockSpec(memory_space=pl.ANY)] * 5,
        out_specs=[vmem] * 3,
        out_shape=[
            jax.ShapeDtypeStruct((CAP_L, head_width), jnp.bfloat16),
            jax.ShapeDtypeStruct((share, HD), jnp.float32),
            jax.ShapeDtypeStruct((share, HD), jnp.float32),
        ],
        scratch_shapes=[
            bf16(rows, width), bf16(rows, head_width), bf16(rows, head_width), bf16(depth, 2 * HD),
            bf16(8 * BLOCK, rows), bf16(CAP_L, CAP_L + HALF),
            bf16(2, HALF, width), bf16(2, 2 * heads, HALF, HD), bf16(HALF, width), bf16(2 * heads, HALF, HD),
            bf16(owners, CAP_L, width), bf16(2 * heads, CAP_L, HD), f32(HALF, 2 * HD), f32(HALF, HD),
            bf16(CAP_L, head_width), bf16(BLOCK, head_width), bf16(HALF, head_width),
            bf16(2, 2 * HD, count * HALF), bf16(2, count, owners, HALF // owners, share), f32(2 * HD, share),
            sems(5), sems(2, CHUNKS + 1), sems(CHUNKS + 1), sems(2, 3, CHUNKS), sems(2, 3, CHUNKS),
            sems(2, count), sems(2, count), sems(2, 3, count), sems(2, 3, count),
            sems(2, count), sems(2, count), sems(2, count), sems(2), sems(2),
        ],
        compiler_params=pltpu.CompilerParams(
            collective_id=0, has_side_effects=True, vmem_limit_bytes=40 * 1024 * 1024
        ),
    )(*(
        pltpu.with_memory_space_constraint(array, pltpu.HBM)
        for array in (lengths, advantage, hidden, queries, upstream, key_weight, value_weight)
    ))


def solution(mesh):
    in_specs = (P("dp", "mp"), P("dp", "mp"), P("dp", "mp"), P(None, "mp"), P(None, "mp"), P(), P())
    out_specs = (P("dp", "mp"), P("dp", "mp"), P("dp", "mp"))
    return jax.shard_map(body, mesh=mesh, in_specs=in_specs, out_specs=out_specs, check_vma=False)
```

```python
import functools

import jax
import jax.numpy as jnp
from jax import lax
from jax.experimental import pallas as pl
from jax.experimental.pallas import tpu as pltpu
from jax.sharding import PartitionSpec as P

HD = 128
BLOCK = 64
HALF = 2 * BLOCK
CAP_L = 4 * BLOCK
CHUNKS = 4

epsilon = 1e-06
masked_score = -1e30
mesh_id = pl.DeviceIdType.MESH
across = (((1,), (1,)), ((), ()))
down = (((0,), (0,)), ((), ()))


def dot32(a, b):
    return jnp.dot(a, b, preferred_element_type=jnp.float32)


def flag(condition):
    return jnp.where(condition, 1, 0).astype(jnp.int32)


def device_facts(lengths, d):
    slots = lengths.shape[1]
    used = jnp.int32(0)
    for r in range(slots):
        used += flag(lengths[d, r] > 0)
    heavy = flag(used >= 6)
    return used, heavy, heavy * ((used - 4) // 2)


def slot_length(lengths, d, slot, valid):
    return jnp.where(valid > 0, lengths[d, jnp.minimum(slot, lengths.shape[1] - 1)], 0)


def slot_start(lengths, d, slot):
    start = jnp.int32(0)
    for r in range(lengths.shape[1]):
        start += jnp.where(r < slot, lengths[d, r], 0)
    return start


def fused_kernel(count, lengths, advantage, hidden_hbm, query_hbm, upstream_hbm, key_hbm, value_hbm,
                 out_ref, key_grad_ref, value_grad_ref,
                 hidden_ref, query_ref, upstream_ref, weight_ref, pick_ref, place_ref,
                 piece_h, piece_qu, inc_h, inc_qu, full, qu, kv_acc, squares, out_buf, out_right_buf, out_in,
                 cots_ref, slices, acc,
                 local_done, piece_sent, piece_got, mp_sent, mp_got, s1_sent, s1_got, s2_sent, s2_got,
                 cot_sent, cot_passed, cot_got, out_sent, out_got):
    me, m = lax.axis_index("dp"), lax.axis_index("mp")
    half, core = m // 2, m % 2
    near, far = half * 2 + 1 - core, (1 - half) * 2 + core
    owners, _, width = full.shape
    chunk = width // CHUNKS
    heads = query_ref.shape[1] // HD
    share = slices.shape[4]
    per = width // share
    part = HALF // owners
    place = me % 4
    middle = (place == 1) | (place == 2)
    has_left, has_right = me > 0, me < count - 1
    line, side_y, lines = me // 2, me % 2, count // 2
    partner = line * 2 + 1 - side_y

    fetches = [
        pltpu.make_async_copy(source, target, local_done.at[n])
        for n, (source, target) in enumerate((
            (hidden_hbm, hidden_ref),
            (query_hbm, query_ref),
            (upstream_hbm, upstream_ref),
            (key_hbm, weight_ref.at[:, :HD]),
            (value_hbm, weight_ref.at[:, HD:]),
        ))
    ]

    def piece_copy(side, p):
        if p < CHUNKS:
            columns = slice(p * chunk, (p + 1) * chunk)
            source, target = piece_h.at[side, :, columns], inc_h.at[:, columns]
        else:
            source, target = piece_qu.at[side], inc_qu
        return pltpu.make_async_remote_copy(
            src_ref=source, dst_ref=target, send_sem=piece_sent.at[side, p], recv_sem=piece_got.at[p],
            device_id={"dp": me + 2 * side - 1}, device_id_type=mesh_id,
        )

    def over_mp(h, kind, c):
        owner, target = (m, near) if kind == 0 else (m, far) if kind <= 2 else (far, near)
        first = h * HALF
        if kind > 0:
            sub = half if kind in (2, 3) else 1 - half
            first = pl.multiple_of(first + sub * BLOCK, BLOCK)
        rows = pl.ds(first, HALF if kind == 0 else BLOCK)
        spot = full.at[owner, rows, c * chunk : (c + 1) * chunk]
        return pltpu.make_async_remote_copy(
            src_ref=spot, dst_ref=spot, send_sem=mp_sent.at[h, kind, c], recv_sem=mp_got.at[h, kind, c],
            device_id={"mp": target}, device_id_type=mesh_id,
        )

    def slice_out(h, j):
        rows = pl.ds(pl.multiple_of(h * HALF + m * part, part), part)
        columns = pl.ds(pl.multiple_of(j % per * share, share), share)
        return pltpu.make_async_remote_copy(
            src_ref=full.at[j // per, rows, columns], dst_ref=slices.at[h, me, m],
            send_sem=s1_sent.at[h, j], recv_sem=s1_got.at[h, me],
            device_id={"dp": j}, device_id_type=mesh_id,
        )

    def slice_in(h, j):
        return pltpu.make_async_remote_copy(
            src_ref=slices.at[h, j, m], dst_ref=slices.at[h, j, m],
            send_sem=s1_sent.at[h, j], recv_sem=s1_got.at[h, j],
            device_id={"dp": j}, device_id_type=mesh_id,
        )

    def slices_mp(h, kind, i):
        owner, target = ((m, near), (m, far), (far, near))[kind]
        spot = slices.at[h, i, owner]
        return pltpu.make_async_remote_copy(
            src_ref=spot, dst_ref=spot, send_sem=s2_sent.at[h, kind, i], recv_sem=s2_got.at[h, kind, i],
            device_id={"mp": target}, device_id_type=mesh_id,
        )

    def cots_of(h, d):
        return cots_ref.at[h, :, pl.ds(pl.multiple_of(d * HALF, HALF), HALF)]

    def cot_out(h, j):
        return pltpu.make_async_remote_copy(
            src_ref=cots_of(h, me), dst_ref=cots_of(h, me), send_sem=cot_sent.at[h, j], recv_sem=cot_got.at[h, me],
            device_id={"dp": j}, device_id_type=mesh_id,
        )

    def cot_on(h, j):
        return pltpu.make_async_remote_copy(
            src_ref=cots_of(h, j), dst_ref=cots_of(h, j), send_sem=cot_passed.at[h, j], recv_sem=cot_got.at[h, j],
            device_id={"dp": partner}, device_id_type=mesh_id,
        )

    def out_copy(side):
        source, target = (out_buf.at[:BLOCK], out_in.at[BLOCK:]) if side == 0 else (out_right_buf, out_in.at[:BLOCK])
        return pltpu.make_async_remote_copy(
            src_ref=source, dst_ref=target, send_sem=out_sent.at[side], recv_sem=out_got.at[side],
            device_id={"dp": me + 2 * side - 1}, device_id_type=mesh_id,
        )

    gives_left = has_left & (place != 2)
    gives_right = has_right & (place != 1)
    takes_left = has_left & (place != 2)
    takes_right = has_right & (place != 1)

    def others(body):
        @pl.loop(1, count)
        def _(k):
            body(lax.rem(me + k, count))

    def along_line(body):
        @pl.loop(1, lines)
        def _(k):
            body(lax.rem(line + k, lines) * 2 + side_y)

    def send_slices(h, block, first, last):
        @pl.loop(first, last)
        def _(e):
            j = block * per + e

            @pl.when(j != me)
            def _():
                slice_out(h, j).start()

    def finished(c):
        return max(c * chunk // share, 0), (c + 1) * chunk // share

    def send_cots(h):
        if h == 1:
            others(lambda j: cot_out(h, j).start())
            return
        along_line(lambda j: cot_out(h, j).start())
        cot_out(h, partner).start()

    def pass_cot(h, j):
        cot_on(h, j).wait_recv()
        cot_on(h, j).start()

    def pass_cots(h):
        along_line(lambda j: pass_cot(h, j))

    def slices_on(h, i):
        slice_in(h, i).wait_recv()
        slices_mp(h, 1, i).start()
        slices_mp(h, 0, i).start()

    def send_over_mp(h):
        others(lambda i: slices_on(h, i))

    def relay_over_mp(h):
        def one(i):
            slices_mp(h, 1, i).wait_recv()
            slices_mp(h, 2, i).start()

        others(one)

    for fetch in fetches:
        fetch.start()
    barrier = pltpu.get_barrier_semaphore()
    for target in (near, far):
        pl.semaphore_signal(barrier, inc=1, device_id={"mp": target}, device_id_type=mesh_id)
    others(lambda j: pl.semaphore_signal(barrier, inc=1, device_id={"dp": j}, device_id_type=mesh_id))

    source = jnp.where(place <= 1, me + 1, me - 1)
    used, heavy, left_slots = device_facts(lengths, me)
    s_used, s_heavy, s_left = device_facts(lengths, source)
    kept = jnp.where(heavy > 0, 4, used)
    wanted = []
    for b in range(4):
        wanted.append((left_slots + b, flag(b < kept)))
    for b in range(2):
        wanted.append((jnp.int32(b), heavy * flag(b < left_slots)))
    for b in range(2):
        slot = left_slots + 4 + b
        wanted.append((slot, heavy * flag(slot < used)))
    sizes = [slot_length(lengths, me, slot, valid) for slot, valid in wanted]
    own_sizes = sizes[:4]
    own_rates = [advantage[me, jnp.minimum(slot, lengths.shape[1] - 1)] for slot, _ in wanted[:4]]
    in_sizes, in_rates = [], []
    for b in range(2):
        slot = jnp.where(place <= 1, b, s_left + 4 + b)
        valid = s_heavy * jnp.where(place <= 1, flag(b < s_left), flag(slot < s_used))
        in_sizes.append(slot_length(lengths, source, slot, valid))
        in_rates.append(advantage[source, jnp.minimum(slot, lengths.shape[1] - 1)])
    block_sizes = own_sizes[:2] + [own_sizes[2 + b] + in_sizes[b] for b in range(2)]
    block_rates = own_rates[:2] + [jnp.where(in_sizes[b] > 0, in_rates[b], own_rates[2 + b]) for b in range(2)]

    row_of = lax.broadcasted_iota(jnp.int32, (BLOCK, hidden_ref.shape[0]), 0)
    ahead = lax.broadcasted_iota(jnp.int32, (BLOCK, hidden_ref.shape[0]), 1) - row_of
    for b, (slot, _) in enumerate(wanted):
        hit = (ahead == slot_start(lengths, me, slot)) & (row_of < sizes[b])
        pick_ref[b * BLOCK : (b + 1) * BLOCK] = jnp.where(hit, 1.0, 0.0).astype(jnp.bfloat16)

    pl.semaphore_wait(barrier, count + 1)

    fetches[0].wait()
    for c in range(CHUNKS):
        columns = slice(c * chunk, (c + 1) * chunk)

        @pl.when(middle)
        def _():
            both = dot32(pick_ref[CAP_L:], hidden_ref[:, columns]).astype(jnp.bfloat16)
            for side in range(2):
                piece_h[side, :, columns] = both[side * HALF : (side + 1) * HALF]
                piece_copy(side, c).start()

        full[m, :HALF, columns] = dot32(pick_ref[:HALF], hidden_ref[:, columns]).astype(jnp.bfloat16)
        over_mp(0, 1, c).start()
        over_mp(0, 0, c).start()

    for c in range(CHUNKS):
        over_mp(0, 2, c).start()
    fetches[1].wait()
    fetches[2].wait()

    def spread(rows, store):
        for base, array in ((0, query_ref), (heads, upstream_ref)):
            for at in range(0, heads, 4):
                picked = dot32(pick_ref[rows], array[:, at * HD : (at + 4) * HD]).astype(jnp.bfloat16)
                for h in range(4):
                    store(base + at + h, picked[:, h * HD : (h + 1) * HD])

    @pl.when(middle)
    def _():
        def store(h, values):
            piece_qu[0, h] = values[:HALF]
            piece_qu[1, h] = values[HALF:]

        spread(slice(CAP_L, 2 * CAP_L), store)

    @pl.when(middle)
    def _():
        for side in range(2):
            piece_copy(side, CHUNKS).start()

    def store_own(h, values):
        qu[h] = values

    def near_slices(h):
        send_slices(h, m, 0, per)
        for c in range(CHUNKS):
            over_mp(h, 0, c).wait_recv()
        send_slices(h, near, 0, per)

    spread(slice(0, CAP_L), store_own)
    fetches[3].wait()
    fetches[4].wait()

    def absorb(h, c):
        total = jnp.zeros(kv_acc.shape, jnp.float32) if c == 0 else kv_acc[...]
        squared = jnp.zeros(squares.shape, jnp.float32) if c == 0 else squares[...]
        for owner in range(owners):
            block = full[owner, h * HALF : (h + 1) * HALF, c * chunk : (c + 1) * chunk]
            spot = owner * width + c * chunk
            total += dot32(block, weight_ref[spot : spot + chunk])
            for at in range(0, chunk, HD):
                wide = block[:, at : at + HD].astype(jnp.float32)
                squared += wide * wide
        kv_acc[...] = total
        squares[...] = squared

    corner = (1 - half) * 2 + 1 - core

    def pass_first(h, c):
        over_mp(h, 1, c).wait_recv()
        over_mp(h, 3, c).start()

    def slice_first(h, c):
        over_mp(h, 3, c).wait_recv()
        first, last = finished(c)
        if last > first:
            for block in (far, corner):
                send_slices(h, block, first, last)

    def pass_rest(h):
        for c in range(CHUNKS):
            over_mp(h, 2, c).wait_recv()
            over_mp(h, 4, c).start()
            if c > 0:
                over_mp(h, 4, c - 1).wait_recv()
                absorb(h, c - 1)

    def absorb_last(h):
        over_mp(h, 4, CHUNKS - 1).wait_recv()
        absorb(h, CHUNKS - 1)

    for c in range(CHUNKS):
        columns = slice(c * chunk, (c + 1) * chunk)
        pass_first(0, c)
        own = dot32(pick_ref[HALF:CAP_L], hidden_ref[:, columns])
        piece_copy(0, c).wait_recv()
        full[m, HALF:, columns] = (own + inc_h[:, columns].astype(jnp.float32)).astype(jnp.bfloat16)
        over_mp(1, 1, c).start()
        over_mp(1, 0, c).start()
        slice_first(0, c)
    for c in range(CHUNKS):
        over_mp(1, 2, c).start()
    near_slices(0)
    pass_rest(0)
    absorb_last(0)

    def local_slice(h):
        columns = pl.ds(pl.multiple_of(me % per * share, share), share)
        slices[h, me] = full[me // per, h * HALF : (h + 1) * HALF, columns].reshape(owners, part, share)

    def attend(h):
        scale = lax.rsqrt(jnp.sum(squares[...], axis=1, keepdims=True) / (owners * width) + epsilon)
        keys_values = (kv_acc[...] * scale).astype(jnp.bfloat16)
        inverse_root = HD ** (-0.5)
        u = lax.broadcasted_iota(jnp.int32, (BLOCK, heads * BLOCK), 0)
        t = lax.broadcasted_iota(jnp.int32, (BLOCK, heads * BLOCK), 1) % BLOCK
        allowed = u <= t
        row = lax.broadcasted_iota(jnp.int32, (BLOCK, HD), 0)
        terms = []
        for b in range(2):
            block = 2 * h + b
            rows = slice(block * BLOCK, (block + 1) * BLOCK)
            key, value = (keys_values[b * BLOCK : (b + 1) * BLOCK, at : at + HD] for at in (0, HD))
            size = jnp.full((BLOCK, HD), block_sizes[block], jnp.int32)
            rate = jnp.full((BLOCK, HD), block_rates[block], jnp.float32) / jnp.maximum(size, 1).astype(jnp.float32)
            rate = jnp.where(row < size, rate, 0.0)
            query = qu[:heads, rows].reshape(heads * BLOCK, HD)
            cot = (qu[heads:, rows].astype(jnp.float32) * rate[None]).astype(jnp.bfloat16).reshape(heads * BLOCK, HD)
            scores = lax.dot_general(key, query, across, preferred_element_type=jnp.float32) * inverse_root
            scores = jnp.where(allowed, scores, masked_score)
            raised = jnp.exp(scores - jnp.max(scores, axis=0, keepdims=True))
            probability = raised * (1.0 / jnp.sum(raised, axis=0, keepdims=True))
            weights = probability.astype(jnp.bfloat16)
            attended = lax.dot_general(weights, value, down, preferred_element_type=jnp.float32).astype(jnp.bfloat16)
            for q in range(heads):
                out_buf[rows, q * HD : (q + 1) * HD] = attended[q * BLOCK : (q + 1) * BLOCK]
            prob_grad = lax.dot_general(value, cot, across, preferred_element_type=jnp.float32)
            centre = jnp.sum(probability * prob_grad, axis=0, keepdims=True)
            score_grad = (probability * (prob_grad - centre)).astype(jnp.bfloat16)
            key_cot = dot32(score_grad, query) * inverse_root
            value_cot = dot32(weights, cot)
            terms.append(jnp.concatenate([key_cot, value_cot], axis=1))
        cots = jnp.concatenate(terms, axis=0) * scale
        cots_ref[h, :, pl.ds(pl.multiple_of(me * HALF, HALF), HALF)] = cots.T.astype(jnp.bfloat16)

    attend(0)
    send_cots(0)
    near_slices(1)
    local_slice(0)

    @pl.when(gives_left)
    def _():
        out_copy(0).start()

    for c in range(CHUNKS):
        pass_first(1, c)
        if c > 0:
            slice_first(1, c - 1)
    slice_first(1, CHUNKS - 1)
    pass_rest(1)
    send_over_mp(0)
    absorb_last(1)
    piece_copy(0, CHUNKS).wait_recv()
    for h in range(2 * heads):
        qu[h, HALF:] = (qu[h, HALF:].astype(jnp.float32) + inc_qu[h].astype(jnp.float32)).astype(jnp.bfloat16)
    attend(1)
    send_cots(1)
    pass_cots(0)
    local_slice(1)

    no_left = flag(has_left) * (1 - device_facts(lengths, jnp.maximum(me - 1, 0))[1])
    sends_two = jnp.full((BLOCK, out_buf.shape[1]), no_left, jnp.int32) > 0
    out_right_buf[...] = jnp.where(
        sends_two, out_buf[HALF : HALF + BLOCK].astype(jnp.float32), out_buf[BLOCK:HALF].astype(jnp.float32)
    ).astype(jnp.bfloat16)

    @pl.when(gives_right)
    def _():
        out_copy(1).start()

    @pl.when(jnp.logical_not(takes_left))
    def _():
        out_in[:BLOCK] = jnp.zeros((BLOCK, out_in.shape[1]), jnp.bfloat16)

    @pl.when(jnp.logical_not(takes_right))
    def _():
        out_in[BLOCK:] = jnp.zeros((BLOCK, out_in.shape[1]), jnp.bfloat16)

    def one_line(j):
        for i in (j, j // 2 * 2 + 1 - side_y):
            slices_on(1, i)

    slices_on(1, partner)
    along_line(one_line)
    relay_over_mp(0)

    heavy_left = flag(has_left) * device_facts(lengths, jnp.maximum(me - 1, 0))[1]
    heavy_right = flag(has_right) * device_facts(lengths, jnp.minimum(me + 1, count - 1))[1]
    light = 1 - heavy
    gives = flag(has_left) * (1 - heavy_left)
    second = flag(me > 1) * (1 - device_facts(lengths, jnp.maximum(me - 2, 0))[1])
    from_left = light * flag(has_left) * (1 - heavy_left) * lengths[jnp.maximum(me - 1, 0), second + 1]
    from_right = light * flag(has_right) * (1 - heavy_right) * lengths[jnp.minimum(me + 1, count - 1), 0]
    total_in = in_sizes[0] + in_sizes[1]
    kept_size = lengths[me, gives]
    base_kept = from_left + heavy_left * total_in
    base_in = jnp.where(heavy_left > 0, 0, base_kept + kept_size)
    base_right = base_kept + kept_size + heavy_right * total_in
    spots = []
    running = jnp.int32(0)
    for b in range(4):
        if b < 2:
            size, at = jnp.where(gives == b, kept_size, 0), base_kept
        else:
            size, at = in_sizes[b - 2], base_in + (in_sizes[0] if b == 3 else 0)
        spots.append((jnp.where(heavy > 0, running, at), jnp.where(heavy > 0, own_sizes[b], size)))
        running = running + own_sizes[b]
    spots += [(jnp.int32(0), from_left), (base_right, from_right)]
    target = lax.broadcasted_iota(jnp.int32, (CAP_L, HALF), 0)
    lane = lax.broadcasted_iota(jnp.int32, (CAP_L, HALF), 1)
    first = lane < BLOCK
    offset = lane % BLOCK
    for pair in range(3):
        (at0, size0), (at1, size1) = spots[2 * pair : 2 * pair + 2]
        at = jnp.where(first, at0, at1)
        size = jnp.where(first, size0, size1)
        hit = (target - at == offset) & (offset < size)
        place_ref[:, pair * HALF : (pair + 1) * HALF] = jnp.where(hit, 1.0, 0.0).astype(jnp.bfloat16)

    @pl.when(takes_left)
    def _():
        out_copy(1).wait_recv()

    @pl.when(takes_right)
    def _():
        out_copy(0).wait_recv()

    for at in range(0, out_ref.shape[1], 256):
        columns = slice(at, at + 256)
        total = dot32(place_ref[:, :CAP_L], out_buf[:, columns]) + dot32(place_ref[:, CAP_L:], out_in[:, columns])
        out_ref[:, columns] = total.astype(jnp.bfloat16)

    for h in range(2):
        if h == 1:
            relay_over_mp(1)

        def gathered(i):
            slices_mp(h, 0, i).wait_recv()
            slices_mp(h, 2, i).wait_recv()

        others(gathered)
        if h == 1:
            others(lambda j: cot_on(h, j).wait_recv())
        else:
            cot_on(h, partner).wait_recv()
            along_line(lambda j: cot_on(h, j // 2 * 2 + 1 - side_y).wait_recv())
        tile = min(256, share)
        for at in range(0, share, tile):
            columns = slice(at, at + tile)
            rows = slices[h, :, :, :, columns].reshape(count * HALF, tile)
            term = dot32(cots_ref[h], rows)
            if h == 0:
                acc[:, columns] = term
            else:
                acc[:, columns] += term
    key_grad_ref[...] = acc[:HD].T
    value_grad_ref[...] = acc[HD:].T

    @pl.when(middle)
    def _():
        for side in range(2):
            for p in range(CHUNKS + 1):
                piece_copy(side, p).wait_send()

    @pl.when(gives_left)
    def _():
        out_copy(0).wait_send()

    @pl.when(gives_right)
    def _():
        out_copy(1).wait_send()

    for h in range(2):
        for kind in range(5):
            for c in range(CHUNKS):
                over_mp(h, kind, c).wait_send()

        def left(j):
            slice_out(h, j).wait_send()
            for kind in range(3):
                slices_mp(h, kind, j).wait_send()

        def passed(j):
            cot_out(h, j).wait_send()
            cot_on(h, j).wait_send()

        others(left)
        if h == 1:
            others(lambda j: cot_out(h, j).wait_send())
        else:
            along_line(passed)
            cot_out(h, partner).wait_send()


def write_kernel(*refs):
    inputs, outputs, done = refs[:3], refs[3:6], refs[6]
    copies = [pltpu.make_async_copy(a, b, done.at[n]) for n, (a, b) in enumerate(zip(inputs, outputs))]
    for copy in copies:
        copy.start()
    for copy in copies:
        copy.wait()


def write_out(*arrays):
    return pl.pallas_call(
        write_kernel,
        in_specs=[pl.BlockSpec(memory_space=pltpu.VMEM)] * 3,
        out_specs=[pl.BlockSpec(memory_space=pltpu.HBM)] * 3,
        out_shape=[jax.ShapeDtypeStruct(array.shape, array.dtype) for array in arrays],
        scratch_shapes=[pltpu.SemaphoreType.DMA((3,))],
        compiler_params=pltpu.CompilerParams(vmem_limit_bytes=8 * 1024 * 1024),
    )(*arrays)


def body(hidden, queries, upstream, key_weight, value_weight, lengths, advantage):
    count, owners = lax.axis_size("dp"), lax.axis_size("mp")
    rows, width = hidden.shape
    head_width = queries.shape[1]
    heads = head_width // HD
    depth = key_weight.shape[0]
    share = depth // count
    vmem = pl.BlockSpec(memory_space=pltpu.VMEM)
    smem = pl.BlockSpec(memory_space=pltpu.SMEM)
    bf16 = lambda *shape: pltpu.VMEM(shape, jnp.bfloat16)
    f32 = lambda *shape: pltpu.VMEM(shape, jnp.float32)
    sems = lambda *shape: pltpu.SemaphoreType.DMA(shape)
    results = pl.pallas_call(
        functools.partial(fused_kernel, count),
        in_specs=[smem] * 2 + [pl.BlockSpec(memory_space=pl.ANY)] * 5,
        out_specs=[vmem] * 3,
        out_shape=[
            jax.ShapeDtypeStruct((CAP_L, head_width), jnp.bfloat16),
            jax.ShapeDtypeStruct((share, HD), jnp.float32),
            jax.ShapeDtypeStruct((share, HD), jnp.float32),
        ],
        scratch_shapes=[
            bf16(rows, width), bf16(rows, head_width), bf16(rows, head_width), bf16(depth, 2 * HD),
            bf16(8 * BLOCK, rows), bf16(CAP_L, CAP_L + HALF),
            bf16(2, HALF, width), bf16(2, 2 * heads, HALF, HD), bf16(HALF, width), bf16(2 * heads, HALF, HD),
            bf16(owners, CAP_L, width), bf16(2 * heads, CAP_L, HD), f32(HALF, 2 * HD), f32(HALF, HD),
            bf16(CAP_L, head_width), bf16(BLOCK, head_width), bf16(HALF, head_width),
            bf16(2, 2 * HD, count * HALF), bf16(2, count, owners, HALF // owners, share), f32(2 * HD, share),
            sems(5), sems(2, CHUNKS + 1), sems(CHUNKS + 1), sems(2, 5, CHUNKS), sems(2, 5, CHUNKS),
            sems(2, count), sems(2, count), sems(2, 3, count), sems(2, 3, count),
            sems(2, count), sems(2, count), sems(2, count), sems(2), sems(2),
        ],
        compiler_params=pltpu.CompilerParams(
            collective_id=0, has_side_effects=True, vmem_limit_bytes=40 * 1024 * 1024
        ),
    )(*(
        pltpu.with_memory_space_constraint(array, pltpu.HBM)
        for array in (lengths, advantage, hidden, queries, upstream, key_weight, value_weight)
    ))
    return tuple(write_out(*results))


def solution(mesh):
    in_specs = (P("dp", "mp"), P("dp", "mp"), P("dp", "mp"), P(None, "mp"), P(None, "mp"), P(), P())
    out_specs = (P("dp", "mp"), P("dp", "mp"), P("dp", "mp"))
    return jax.shard_map(body, mesh=mesh, in_specs=in_specs, out_specs=out_specs, check_vma=False)
```

```python
import functools

import jax
import jax.numpy as jnp
from jax import lax
from jax.experimental import pallas as pl
from jax.experimental.pallas import tpu as pltpu
from jax.sharding import PartitionSpec as P

HD = 128
BLOCK = 64
HALF = 2 * BLOCK
CAP_L = 4 * BLOCK
CHUNKS = 4

epsilon = 1e-06
masked_score = -1e30
mesh_id = pl.DeviceIdType.MESH
across = (((1,), (1,)), ((), ()))
down = (((0,), (0,)), ((), ()))


def dot32(a, b):
    return jnp.dot(a, b, preferred_element_type=jnp.float32)


def flag(condition):
    return jnp.where(condition, 1, 0).astype(jnp.int32)


def device_facts(lengths, d):
    slots = lengths.shape[1]
    used = jnp.int32(0)
    for r in range(slots):
        used += flag(lengths[d, r] > 0)
    heavy = flag(used >= 6)
    return used, heavy, heavy * ((used - 4) // 2)


def slot_length(lengths, d, slot, valid):
    return jnp.where(valid > 0, lengths[d, jnp.minimum(slot, lengths.shape[1] - 1)], 0)


def slot_start(lengths, d, slot):
    start = jnp.int32(0)
    for r in range(lengths.shape[1]):
        start += jnp.where(r < slot, lengths[d, r], 0)
    return start


def fused_kernel(count, lengths, advantage, hidden_hbm, query_hbm, upstream_hbm, key_hbm, value_hbm,
                 out_ref, key_grad_ref, value_grad_ref,
                 hidden_ref, query_ref, upstream_ref, weight_ref, pick_ref, place_ref,
                 piece_h, piece_qu, inc_h, inc_qu, full, qu, kv_acc, squares, out_buf, out_right_buf, out_in,
                 cots_ref, slices, acc,
                 local_done, piece_sent, piece_got, mp_sent, mp_got, s1_sent, s1_got, s2_sent, s2_got,
                 cot_sent, cot_passed, cot_got, out_sent, out_got):
    me, m = lax.axis_index("dp"), lax.axis_index("mp")
    half, core = m // 2, m % 2
    near, far = half * 2 + 1 - core, (1 - half) * 2 + core
    owners, _, width = full.shape
    chunk = width // CHUNKS
    heads = query_ref.shape[1] // HD
    share = slices.shape[4]
    per = width // share
    part = HALF // owners
    place = me % 4
    middle = (place == 1) | (place == 2)
    has_left, has_right = me > 0, me < count - 1
    line, side_y, lines = me // 2, me % 2, count // 2
    partner = line * 2 + 1 - side_y

    fetches = [
        pltpu.make_async_copy(source, target, local_done.at[n])
        for n, (source, target) in enumerate((
            (hidden_hbm, hidden_ref),
            (query_hbm, query_ref),
            (upstream_hbm, upstream_ref),
            (key_hbm, weight_ref.at[:, :HD]),
            (value_hbm, weight_ref.at[:, HD:]),
        ))
    ]

    def piece_copy(side, p):
        if p < CHUNKS:
            columns = slice(p * chunk, (p + 1) * chunk)
            source, target = piece_h.at[side, :, columns], inc_h.at[:, columns]
        else:
            source, target = piece_qu.at[side], inc_qu
        return pltpu.make_async_remote_copy(
            src_ref=source, dst_ref=target, send_sem=piece_sent.at[side, p], recv_sem=piece_got.at[p],
            device_id={"dp": me + 2 * side - 1}, device_id_type=mesh_id,
        )

    def over_mp(h, kind, c):
        owner, target = (m, near) if kind == 0 else (m, far) if kind <= 2 else (far, near)
        first = h * HALF
        if kind > 0:
            sub = half if kind in (2, 3) else 1 - half
            first = pl.multiple_of(first + sub * BLOCK, BLOCK)
        rows = pl.ds(first, HALF if kind == 0 else BLOCK)
        spot = full.at[owner, rows, c * chunk : (c + 1) * chunk]
        return pltpu.make_async_remote_copy(
            src_ref=spot, dst_ref=spot, send_sem=mp_sent.at[h, kind, c], recv_sem=mp_got.at[h, kind, c],
            device_id={"mp": target}, device_id_type=mesh_id,
        )

    def slice_out(h, j):
        rows = pl.ds(pl.multiple_of(h * HALF + m * part, part), part)
        columns = pl.ds(pl.multiple_of(j % per * share, share), share)
        return pltpu.make_async_remote_copy(
            src_ref=full.at[j // per, rows, columns], dst_ref=slices.at[h, me, m],
            send_sem=s1_sent.at[h, j], recv_sem=s1_got.at[h, me],
            device_id={"dp": j}, device_id_type=mesh_id,
        )

    def slice_in(h, j):
        return pltpu.make_async_remote_copy(
            src_ref=slices.at[h, j, m], dst_ref=slices.at[h, j, m],
            send_sem=s1_sent.at[h, j], recv_sem=s1_got.at[h, j],
            device_id={"dp": j}, device_id_type=mesh_id,
        )

    def slices_mp(h, kind, i):
        owner, target = ((m, near), (m, far), (far, near))[kind]
        spot = slices.at[h, i, owner]
        return pltpu.make_async_remote_copy(
            src_ref=spot, dst_ref=spot, send_sem=s2_sent.at[h, kind, i], recv_sem=s2_got.at[h, kind, i],
            device_id={"mp": target}, device_id_type=mesh_id,
        )

    def cots_of(h, d):
        return cots_ref.at[h, :, pl.ds(pl.multiple_of(d * HALF, HALF), HALF)]

    def cot_out(h, j):
        return pltpu.make_async_remote_copy(
            src_ref=cots_of(h, me), dst_ref=cots_of(h, me), send_sem=cot_sent.at[h, j], recv_sem=cot_got.at[h, me],
            device_id={"dp": j}, device_id_type=mesh_id,
        )

    def cot_on(h, j):
        return pltpu.make_async_remote_copy(
            src_ref=cots_of(h, j), dst_ref=cots_of(h, j), send_sem=cot_passed.at[h, j], recv_sem=cot_got.at[h, j],
            device_id={"dp": partner}, device_id_type=mesh_id,
        )

    def out_copy(side):
        source, target = (out_buf.at[:BLOCK], out_in.at[BLOCK:]) if side == 0 else (out_right_buf, out_in.at[:BLOCK])
        return pltpu.make_async_remote_copy(
            src_ref=source, dst_ref=target, send_sem=out_sent.at[side], recv_sem=out_got.at[side],
            device_id={"dp": me + 2 * side - 1}, device_id_type=mesh_id,
        )

    gives_left = has_left & (place != 2)
    gives_right = has_right & (place != 1)
    takes_left = has_left & (place != 2)
    takes_right = has_right & (place != 1)

    def others(body):
        @pl.loop(1, count)
        def _(k):
            body(lax.rem(me + k, count))

    def along_line(body):
        @pl.loop(1, lines)
        def _(k):
            body(lax.rem(line + k, lines) * 2 + side_y)

    def send_slices(h, block, first, last):
        @pl.loop(first, last)
        def _(e):
            j = block * per + e

            @pl.when(j != me)
            def _():
                slice_out(h, j).start()

    def finished(c):
        return max(c * chunk // share, 0), (c + 1) * chunk // share

    def send_cots(h):
        if h == 1:
            others(lambda j: cot_out(h, j).start())
            return
        along_line(lambda j: cot_out(h, j).start())
        cot_out(h, partner).start()

    def pass_cot(h, j):
        cot_on(h, j).wait_recv()
        cot_on(h, j).start()

    def pass_cots(h):
        along_line(lambda j: pass_cot(h, j))

    def slices_on(h, i):
        slice_in(h, i).wait_recv()
        slices_mp(h, 1, i).start()
        slices_mp(h, 0, i).start()

    def send_over_mp(h):
        others(lambda i: slices_on(h, i))

    def relay_over_mp(h):
        def one(i):
            slices_mp(h, 1, i).wait_recv()
            slices_mp(h, 2, i).start()

        others(one)

    for fetch in fetches:
        fetch.start()
    barrier = pltpu.get_barrier_semaphore()
    for target in (near, far):
        pl.semaphore_signal(barrier, inc=1, device_id={"mp": target}, device_id_type=mesh_id)
    others(lambda j: pl.semaphore_signal(barrier, inc=1, device_id={"dp": j}, device_id_type=mesh_id))

    source = jnp.where(place <= 1, me + 1, me - 1)
    used, heavy, left_slots = device_facts(lengths, me)
    s_used, s_heavy, s_left = device_facts(lengths, source)
    kept = jnp.where(heavy > 0, 4, used)
    wanted = []
    for b in range(4):
        wanted.append((left_slots + b, flag(b < kept)))
    for b in range(2):
        wanted.append((jnp.int32(b), heavy * flag(b < left_slots)))
    for b in range(2):
        slot = left_slots + 4 + b
        wanted.append((slot, heavy * flag(slot < used)))
    sizes = [slot_length(lengths, me, slot, valid) for slot, valid in wanted]
    own_sizes = sizes[:4]
    own_rates = [advantage[me, jnp.minimum(slot, lengths.shape[1] - 1)] for slot, _ in wanted[:4]]
    in_sizes, in_rates = [], []
    for b in range(2):
        slot = jnp.where(place <= 1, b, s_left + 4 + b)
        valid = s_heavy * jnp.where(place <= 1, flag(b < s_left), flag(slot < s_used))
        in_sizes.append(slot_length(lengths, source, slot, valid))
        in_rates.append(advantage[source, jnp.minimum(slot, lengths.shape[1] - 1)])
    block_sizes = own_sizes[:2] + [own_sizes[2 + b] + in_sizes[b] for b in range(2)]
    block_rates = own_rates[:2] + [jnp.where(in_sizes[b] > 0, in_rates[b], own_rates[2 + b]) for b in range(2)]

    row_of = lax.broadcasted_iota(jnp.int32, (BLOCK, hidden_ref.shape[0]), 0)
    ahead = lax.broadcasted_iota(jnp.int32, (BLOCK, hidden_ref.shape[0]), 1) - row_of
    for b, (slot, _) in enumerate(wanted):
        hit = (ahead == slot_start(lengths, me, slot)) & (row_of < sizes[b])
        pick_ref[b * BLOCK : (b + 1) * BLOCK] = jnp.where(hit, 1.0, 0.0).astype(jnp.bfloat16)

    pl.semaphore_wait(barrier, count + 1)

    fetches[0].wait()
    for c in range(CHUNKS):
        columns = slice(c * chunk, (c + 1) * chunk)

        @pl.when(middle)
        def _():
            both = dot32(pick_ref[CAP_L:], hidden_ref[:, columns]).astype(jnp.bfloat16)
            for side in range(2):
                piece_h[side, :, columns] = both[side * HALF : (side + 1) * HALF]
                piece_copy(side, c).start()

        full[m, :HALF, columns] = dot32(pick_ref[:HALF], hidden_ref[:, columns]).astype(jnp.bfloat16)
        over_mp(0, 1, c).start()
        over_mp(0, 0, c).start()

    for c in range(CHUNKS):
        over_mp(0, 2, c).start()
    fetches[1].wait()
    fetches[2].wait()

    def spread(rows, store):
        for base, array in ((0, query_ref), (heads, upstream_ref)):
            for at in range(0, heads, 4):
                picked = dot32(pick_ref[rows], array[:, at * HD : (at + 4) * HD]).astype(jnp.bfloat16)
                for h in range(4):
                    store(base + at + h, picked[:, h * HD : (h + 1) * HD])

    @pl.when(middle)
    def _():
        def store(h, values):
            piece_qu[0, h] = values[:HALF]
            piece_qu[1, h] = values[HALF:]

        spread(slice(CAP_L, 2 * CAP_L), store)

    @pl.when(middle)
    def _():
        for side in range(2):
            piece_copy(side, CHUNKS).start()

    def store_own(h, values):
        qu[h] = values

    def near_slices(h):
        send_slices(h, m, 0, per)
        for c in range(CHUNKS):
            over_mp(h, 0, c).wait_recv()
        send_slices(h, near, 0, per)

    spread(slice(0, CAP_L), store_own)
    fetches[3].wait()
    fetches[4].wait()

    def absorb(h, c):
        total = jnp.zeros(kv_acc.shape, jnp.float32) if c == 0 else kv_acc[...]
        squared = jnp.zeros(squares.shape, jnp.float32) if c == 0 else squares[...]
        for owner in range(owners):
            block = full[owner, h * HALF : (h + 1) * HALF, c * chunk : (c + 1) * chunk]
            spot = owner * width + c * chunk
            total += dot32(block, weight_ref[spot : spot + chunk])
            for at in range(0, chunk, HD):
                wide = block[:, at : at + HD].astype(jnp.float32)
                squared += wide * wide
        kv_acc[...] = total
        squares[...] = squared

    corner = (1 - half) * 2 + 1 - core

    def pass_first(h, c):
        over_mp(h, 1, c).wait_recv()
        over_mp(h, 3, c).start()

    def slice_first(h, c):
        over_mp(h, 3, c).wait_recv()
        first, last = finished(c)
        if last > first:
            for block in (far, corner):
                send_slices(h, block, first, last)

    def pass_rest(h):
        for c in range(CHUNKS):
            over_mp(h, 2, c).wait_recv()
            over_mp(h, 4, c).start()
            if c > 0:
                over_mp(h, 4, c - 1).wait_recv()
                absorb(h, c - 1)

    def absorb_last(h):
        over_mp(h, 4, CHUNKS - 1).wait_recv()
        absorb(h, CHUNKS - 1)

    for c in range(CHUNKS):
        columns = slice(c * chunk, (c + 1) * chunk)
        pass_first(0, c)
        own = dot32(pick_ref[HALF:CAP_L], hidden_ref[:, columns])
        piece_copy(0, c).wait_recv()
        full[m, HALF:, columns] = (own + inc_h[:, columns].astype(jnp.float32)).astype(jnp.bfloat16)
        over_mp(1, 1, c).start()
        over_mp(1, 0, c).start()
        slice_first(0, c)
    for c in range(CHUNKS):
        over_mp(1, 2, c).start()
    near_slices(0)
    pass_rest(0)
    absorb_last(0)

    def local_slice(h):
        columns = pl.ds(pl.multiple_of(me % per * share, share), share)
        slices[h, me] = full[me // per, h * HALF : (h + 1) * HALF, columns].reshape(owners, part, share)

    def attend(h):
        scale = lax.rsqrt(jnp.sum(squares[...], axis=1, keepdims=True) / (owners * width) + epsilon)
        keys_values = (kv_acc[...] * scale).astype(jnp.bfloat16)
        inverse_root = HD ** (-0.5)
        u = lax.broadcasted_iota(jnp.int32, (BLOCK, heads * BLOCK), 0)
        t = lax.broadcasted_iota(jnp.int32, (BLOCK, heads * BLOCK), 1) % BLOCK
        allowed = u <= t
        row = lax.broadcasted_iota(jnp.int32, (BLOCK, HD), 0)
        terms = []
        for b in range(2):
            block = 2 * h + b
            rows = slice(block * BLOCK, (block + 1) * BLOCK)
            key, value = (keys_values[b * BLOCK : (b + 1) * BLOCK, at : at + HD] for at in (0, HD))
            size = jnp.full((BLOCK, HD), block_sizes[block], jnp.int32)
            rate = jnp.full((BLOCK, HD), block_rates[block], jnp.float32) / jnp.maximum(size, 1).astype(jnp.float32)
            rate = jnp.where(row < size, rate, 0.0)
            query = qu[:heads, rows].reshape(heads * BLOCK, HD)
            cot = (qu[heads:, rows].astype(jnp.float32) * rate[None]).astype(jnp.bfloat16).reshape(heads * BLOCK, HD)
            scores = lax.dot_general(key, query, across, preferred_element_type=jnp.float32) * inverse_root
            scores = jnp.where(allowed, scores, masked_score)
            raised = jnp.exp(scores - jnp.max(scores, axis=0, keepdims=True))
            probability = raised * (1.0 / jnp.sum(raised, axis=0, keepdims=True))
            weights = probability.astype(jnp.bfloat16)
            attended = lax.dot_general(weights, value, down, preferred_element_type=jnp.float32).astype(jnp.bfloat16)
            for q in range(heads):
                out_buf[rows, q * HD : (q + 1) * HD] = attended[q * BLOCK : (q + 1) * BLOCK]
            prob_grad = lax.dot_general(value, cot, across, preferred_element_type=jnp.float32)
            centre = jnp.sum(probability * prob_grad, axis=0, keepdims=True)
            score_grad = (probability * (prob_grad - centre)).astype(jnp.bfloat16)
            key_cot = dot32(score_grad, query) * inverse_root
            value_cot = dot32(weights, cot)
            terms.append(jnp.concatenate([key_cot, value_cot], axis=1))
        cots = jnp.concatenate(terms, axis=0) * scale
        cots_ref[h, :, pl.ds(pl.multiple_of(me * HALF, HALF), HALF)] = cots.T.astype(jnp.bfloat16)

    attend(0)
    send_cots(0)
    near_slices(1)
    local_slice(0)

    @pl.when(gives_left)
    def _():
        out_copy(0).start()

    for c in range(CHUNKS):
        pass_first(1, c)
        if c > 0:
            slice_first(1, c - 1)
    slice_first(1, CHUNKS - 1)
    pass_rest(1)
    send_over_mp(0)
    absorb_last(1)
    piece_copy(0, CHUNKS).wait_recv()
    for h in range(2 * heads):
        qu[h, HALF:] = (qu[h, HALF:].astype(jnp.float32) + inc_qu[h].astype(jnp.float32)).astype(jnp.bfloat16)
    attend(1)
    send_cots(1)
    pass_cots(0)
    local_slice(1)

    no_left = flag(has_left) * (1 - device_facts(lengths, jnp.maximum(me - 1, 0))[1])
    sends_two = jnp.full((BLOCK, out_buf.shape[1]), no_left, jnp.int32) > 0
    out_right_buf[...] = jnp.where(
        sends_two, out_buf[HALF : HALF + BLOCK].astype(jnp.float32), out_buf[BLOCK:HALF].astype(jnp.float32)
    ).astype(jnp.bfloat16)

    @pl.when(gives_right)
    def _():
        out_copy(1).start()

    @pl.when(jnp.logical_not(takes_left))
    def _():
        out_in[:BLOCK] = jnp.zeros((BLOCK, out_in.shape[1]), jnp.bfloat16)

    @pl.when(jnp.logical_not(takes_right))
    def _():
        out_in[BLOCK:] = jnp.zeros((BLOCK, out_in.shape[1]), jnp.bfloat16)

    def one_line(j):
        for i in (j, j // 2 * 2 + 1 - side_y):
            slices_on(1, i)

    slices_on(1, partner)
    along_line(one_line)
    relay_over_mp(0)

    heavy_left = flag(has_left) * device_facts(lengths, jnp.maximum(me - 1, 0))[1]
    heavy_right = flag(has_right) * device_facts(lengths, jnp.minimum(me + 1, count - 1))[1]
    light = 1 - heavy
    gives = flag(has_left) * (1 - heavy_left)
    second = flag(me > 1) * (1 - device_facts(lengths, jnp.maximum(me - 2, 0))[1])
    from_left = light * flag(has_left) * (1 - heavy_left) * lengths[jnp.maximum(me - 1, 0), second + 1]
    from_right = light * flag(has_right) * (1 - heavy_right) * lengths[jnp.minimum(me + 1, count - 1), 0]
    total_in = in_sizes[0] + in_sizes[1]
    kept_size = lengths[me, gives]
    base_kept = from_left + heavy_left * total_in
    base_in = jnp.where(heavy_left > 0, 0, base_kept + kept_size)
    base_right = base_kept + kept_size + heavy_right * total_in
    spots = []
    running = jnp.int32(0)
    for b in range(4):
        if b < 2:
            size, at = jnp.where(gives == b, kept_size, 0), base_kept
        else:
            size, at = in_sizes[b - 2], base_in + (in_sizes[0] if b == 3 else 0)
        spots.append((jnp.where(heavy > 0, running, at), jnp.where(heavy > 0, own_sizes[b], size)))
        running = running + own_sizes[b]
    spots += [(jnp.int32(0), from_left), (base_right, from_right)]
    target = lax.broadcasted_iota(jnp.int32, (CAP_L, HALF), 0)
    lane = lax.broadcasted_iota(jnp.int32, (CAP_L, HALF), 1)
    first = lane < BLOCK
    offset = lane % BLOCK
    for pair in range(3):
        (at0, size0), (at1, size1) = spots[2 * pair : 2 * pair + 2]
        at = jnp.where(first, at0, at1)
        size = jnp.where(first, size0, size1)
        hit = (target - at == offset) & (offset < size)
        place_ref[:, pair * HALF : (pair + 1) * HALF] = jnp.where(hit, 1.0, 0.0).astype(jnp.bfloat16)

    def place_out():
        @pl.when(takes_left)
        def _():
            out_copy(1).wait_recv()

        @pl.when(takes_right)
        def _():
            out_copy(0).wait_recv()

        for at in range(0, out_ref.shape[1], 256):
            columns = slice(at, at + 256)
            total = dot32(place_ref[:, :CAP_L], out_buf[:, columns]) + dot32(place_ref[:, CAP_L:], out_in[:, columns])
            out_ref[:, columns] = total.astype(jnp.bfloat16)

    for h in range(2):
        if h == 1:
            relay_over_mp(1)
            place_out()

        def gathered(i):
            slices_mp(h, 0, i).wait_recv()
            slices_mp(h, 2, i).wait_recv()

        others(gathered)
        if h == 1:
            others(lambda j: cot_on(h, j).wait_recv())
        else:
            cot_on(h, partner).wait_recv()
            along_line(lambda j: cot_on(h, j // 2 * 2 + 1 - side_y).wait_recv())
        tile = min(256, share)
        for at in range(0, share, tile):
            columns = slice(at, at + tile)
            rows = slices[h, :, :, :, columns].reshape(count * HALF, tile)
            term = dot32(cots_ref[h], rows)
            if h == 0:
                acc[:, columns] = term
            else:
                acc[:, columns] += term
    key_grad_ref[...] = acc[:HD].T
    value_grad_ref[...] = acc[HD:].T

    @pl.when(middle)
    def _():
        for side in range(2):
            for p in range(CHUNKS + 1):
                piece_copy(side, p).wait_send()

    @pl.when(gives_left)
    def _():
        out_copy(0).wait_send()

    @pl.when(gives_right)
    def _():
        out_copy(1).wait_send()

    for h in range(2):
        for kind in range(5):
            for c in range(CHUNKS):
                over_mp(h, kind, c).wait_send()

        def left(j):
            slice_out(h, j).wait_send()
            for kind in range(3):
                slices_mp(h, kind, j).wait_send()

        def passed(j):
            cot_out(h, j).wait_send()
            cot_on(h, j).wait_send()

        others(left)
        if h == 1:
            others(lambda j: cot_out(h, j).wait_send())
        else:
            along_line(passed)
            cot_out(h, partner).wait_send()


def write_kernel(*refs):
    inputs, outputs, done = refs[:3], refs[3:6], refs[6]
    copies = [pltpu.make_async_copy(a, b, done.at[n]) for n, (a, b) in enumerate(zip(inputs, outputs))]
    for copy in copies:
        copy.start()
    for copy in copies:
        copy.wait()


def write_out(*arrays):
    return pl.pallas_call(
        write_kernel,
        in_specs=[pl.BlockSpec(memory_space=pltpu.VMEM)] * 3,
        out_specs=[pl.BlockSpec(memory_space=pltpu.HBM)] * 3,
        out_shape=[jax.ShapeDtypeStruct(array.shape, array.dtype) for array in arrays],
        scratch_shapes=[pltpu.SemaphoreType.DMA((3,))],
        compiler_params=pltpu.CompilerParams(vmem_limit_bytes=8 * 1024 * 1024),
    )(*arrays)


def body(hidden, queries, upstream, key_weight, value_weight, lengths, advantage):
    count, owners = lax.axis_size("dp"), lax.axis_size("mp")
    rows, width = hidden.shape
    head_width = queries.shape[1]
    heads = head_width // HD
    depth = key_weight.shape[0]
    share = depth // count
    vmem = pl.BlockSpec(memory_space=pltpu.VMEM)
    smem = pl.BlockSpec(memory_space=pltpu.SMEM)
    bf16 = lambda *shape: pltpu.VMEM(shape, jnp.bfloat16)
    f32 = lambda *shape: pltpu.VMEM(shape, jnp.float32)
    sems = lambda *shape: pltpu.SemaphoreType.DMA(shape)
    results = pl.pallas_call(
        functools.partial(fused_kernel, count),
        in_specs=[smem] * 2 + [pl.BlockSpec(memory_space=pl.ANY)] * 5,
        out_specs=[vmem] * 3,
        out_shape=[
            jax.ShapeDtypeStruct((CAP_L, head_width), jnp.bfloat16),
            jax.ShapeDtypeStruct((share, HD), jnp.float32),
            jax.ShapeDtypeStruct((share, HD), jnp.float32),
        ],
        scratch_shapes=[
            bf16(rows, width), bf16(rows, head_width), bf16(rows, head_width), bf16(depth, 2 * HD),
            bf16(8 * BLOCK, rows), bf16(CAP_L, CAP_L + HALF),
            bf16(2, HALF, width), bf16(2, 2 * heads, HALF, HD), bf16(HALF, width), bf16(2 * heads, HALF, HD),
            bf16(owners, CAP_L, width), bf16(2 * heads, CAP_L, HD), f32(HALF, 2 * HD), f32(HALF, HD),
            bf16(CAP_L, head_width), bf16(BLOCK, head_width), bf16(HALF, head_width),
            bf16(2, 2 * HD, count * HALF), bf16(2, count, owners, HALF // owners, share), f32(2 * HD, share),
            sems(5), sems(2, CHUNKS + 1), sems(CHUNKS + 1), sems(2, 5, CHUNKS), sems(2, 5, CHUNKS),
            sems(2, count), sems(2, count), sems(2, 3, count), sems(2, 3, count),
            sems(2, count), sems(2, count), sems(2, count), sems(2), sems(2),
        ],
        compiler_params=pltpu.CompilerParams(
            collective_id=0, has_side_effects=True, vmem_limit_bytes=40 * 1024 * 1024
        ),
    )(*(
        pltpu.with_memory_space_constraint(array, pltpu.HBM)
        for array in (lengths, advantage, hidden, queries, upstream, key_weight, value_weight)
    ))
    return tuple(write_out(*results))


def solution(mesh):
    in_specs = (P("dp", "mp"), P("dp", "mp"), P("dp", "mp"), P(None, "mp"), P(None, "mp"), P(), P())
    out_specs = (P("dp", "mp"), P("dp", "mp"), P("dp", "mp"))
    return jax.shard_map(body, mesh=mesh, in_specs=in_specs, out_specs=out_specs, check_vma=False)
```

```python
import functools

import jax
import jax.numpy as jnp
from jax import lax
from jax.experimental import pallas as pl
from jax.experimental.pallas import tpu as pltpu
from jax.sharding import PartitionSpec as P

HD = 128
BLOCK = 64
HALF = 2 * BLOCK
CAP_L = 4 * BLOCK
CHUNKS = 4

epsilon = 1e-06
masked_score = -1e30
mesh_id = pl.DeviceIdType.MESH
across = (((1,), (1,)), ((), ()))
down = (((0,), (0,)), ((), ()))


def dot32(a, b):
    return jnp.dot(a, b, preferred_element_type=jnp.float32)


def flag(condition):
    return jnp.where(condition, 1, 0).astype(jnp.int32)


def device_facts(lengths, d):
    slots = lengths.shape[1]
    used = jnp.int32(0)
    for r in range(slots):
        used += flag(lengths[d, r] > 0)
    heavy = flag(used >= 6)
    return used, heavy, heavy * ((used - 4) // 2)


def slot_length(lengths, d, slot, valid):
    return jnp.where(valid > 0, lengths[d, jnp.minimum(slot, lengths.shape[1] - 1)], 0)


def slot_start(lengths, d, slot):
    start = jnp.int32(0)
    for r in range(lengths.shape[1]):
        start += jnp.where(r < slot, lengths[d, r], 0)
    return start


def fused_kernel(count, lengths, advantage, hidden_hbm, query_hbm, upstream_hbm, key_hbm, value_hbm,
                 out_ref, key_grad_ref, value_grad_ref,
                 hidden_ref, query_ref, upstream_ref, weight_ref, pick_ref, place_ref,
                 piece_h, piece_qu, inc_h, inc_qu, full, qu, kv_acc, squares, out_buf, out_right_buf, out_in,
                 cots_ref, slices, acc,
                 local_done, piece_sent, piece_got, mp_sent, mp_got, s1_sent, s1_got, s2_sent, s2_got,
                 cot_sent, cot_passed, cot_got, out_sent, out_got):
    me, m = lax.axis_index("dp"), lax.axis_index("mp")
    half, core = m // 2, m % 2
    near, far = half * 2 + 1 - core, (1 - half) * 2 + core
    owners, _, width = full.shape
    chunk = width // CHUNKS
    heads = query_ref.shape[1] // HD
    share = slices.shape[4]
    per = width // share
    part = HALF // owners
    place = me % 4
    middle = (place == 1) | (place == 2)
    has_left, has_right = me > 0, me < count - 1
    line, side_y, lines = me // 2, me % 2, count // 2
    partner = line * 2 + 1 - side_y

    fetches = [
        pltpu.make_async_copy(source, target, local_done.at[n])
        for n, (source, target) in enumerate((
            (hidden_hbm, hidden_ref),
            (query_hbm, query_ref),
            (upstream_hbm, upstream_ref),
            (key_hbm, weight_ref.at[:, :HD]),
            (value_hbm, weight_ref.at[:, HD:]),
        ))
    ]

    def piece_copy(side, p):
        if p < CHUNKS:
            columns = slice(p * chunk, (p + 1) * chunk)
            source, target = piece_h.at[side, :, columns], inc_h.at[:, columns]
        else:
            source, target = piece_qu.at[side], inc_qu
        return pltpu.make_async_remote_copy(
            src_ref=source, dst_ref=target, send_sem=piece_sent.at[side, p], recv_sem=piece_got.at[p],
            device_id={"dp": me + 2 * side - 1}, device_id_type=mesh_id,
        )

    def over_mp(h, kind, c):
        owner, target = (m, near) if kind == 0 else (m, far) if kind <= 2 else (far, near)
        first = h * HALF
        if kind > 0:
            sub = half if kind in (2, 3) else 1 - half
            first = pl.multiple_of(first + sub * BLOCK, BLOCK)
        rows = pl.ds(first, HALF if kind == 0 else BLOCK)
        spot = full.at[owner, rows, c * chunk : (c + 1) * chunk]
        return pltpu.make_async_remote_copy(
            src_ref=spot, dst_ref=spot, send_sem=mp_sent.at[h, kind, c], recv_sem=mp_got.at[h, kind, c],
            device_id={"mp": target}, device_id_type=mesh_id,
        )

    def slice_out(h, j):
        rows = pl.ds(pl.multiple_of(h * HALF + m * part, part), part)
        columns = pl.ds(pl.multiple_of(j % per * share, share), share)
        return pltpu.make_async_remote_copy(
            src_ref=full.at[j // per, rows, columns], dst_ref=slices.at[h, me, m],
            send_sem=s1_sent.at[h, j], recv_sem=s1_got.at[h, me],
            device_id={"dp": j}, device_id_type=mesh_id,
        )

    def slice_in(h, j):
        return pltpu.make_async_remote_copy(
            src_ref=slices.at[h, j, m], dst_ref=slices.at[h, j, m],
            send_sem=s1_sent.at[h, j], recv_sem=s1_got.at[h, j],
            device_id={"dp": j}, device_id_type=mesh_id,
        )

    def slices_mp(h, kind, i):
        owner, target = ((m, near), (m, far), (far, near))[kind]
        spot = slices.at[h, i, owner]
        return pltpu.make_async_remote_copy(
            src_ref=spot, dst_ref=spot, send_sem=s2_sent.at[h, kind, i], recv_sem=s2_got.at[h, kind, i],
            device_id={"mp": target}, device_id_type=mesh_id,
        )

    def cots_of(h, d):
        return cots_ref.at[h, :, pl.ds(pl.multiple_of(d * HALF, HALF), HALF)]

    def cot_out(h, j):
        return pltpu.make_async_remote_copy(
            src_ref=cots_of(h, me), dst_ref=cots_of(h, me), send_sem=cot_sent.at[h, j], recv_sem=cot_got.at[h, me],
            device_id={"dp": j}, device_id_type=mesh_id,
        )

    def cot_on(h, j):
        return pltpu.make_async_remote_copy(
            src_ref=cots_of(h, j), dst_ref=cots_of(h, j), send_sem=cot_passed.at[h, j], recv_sem=cot_got.at[h, j],
            device_id={"dp": partner}, device_id_type=mesh_id,
        )

    def out_copy(side):
        source, target = (out_buf.at[:BLOCK], out_in.at[BLOCK:]) if side == 0 else (out_right_buf, out_in.at[:BLOCK])
        return pltpu.make_async_remote_copy(
            src_ref=source, dst_ref=target, send_sem=out_sent.at[side], recv_sem=out_got.at[side],
            device_id={"dp": me + 2 * side - 1}, device_id_type=mesh_id,
        )

    gives_left = has_left & (place != 2)
    gives_right = has_right & (place != 1)
    takes_left = has_left & (place != 2)
    takes_right = has_right & (place != 1)

    def others(body):
        @pl.loop(1, count)
        def _(k):
            body(lax.rem(me + k, count))

    def along_line(body):
        @pl.loop(1, lines)
        def _(k):
            body(lax.rem(line + k, lines) * 2 + side_y)

    def send_slices(h, block, first, last):
        @pl.loop(first, last)
        def _(e):
            j = block * per + e

            @pl.when(j != me)
            def _():
                slice_out(h, j).start()

    def finished(c):
        return max(c * chunk // share, 0), (c + 1) * chunk // share

    def send_cots(h):
        if h == 1:
            others(lambda j: cot_out(h, j).start())
            return
        along_line(lambda j: cot_out(h, j).start())
        cot_out(h, partner).start()

    def pass_cot(h, j):
        cot_on(h, j).wait_recv()
        cot_on(h, j).start()

    def pass_cots(h):
        along_line(lambda j: pass_cot(h, j))

    def slices_on(h, i):
        slice_in(h, i).wait_recv()
        slices_mp(h, 1, i).start()
        slices_mp(h, 0, i).start()

    def send_over_mp(h):
        others(lambda i: slices_on(h, i))

    def relay_over_mp(h):
        def one(i):
            slices_mp(h, 1, i).wait_recv()
            slices_mp(h, 2, i).start()

        others(one)

    for fetch in fetches:
        fetch.start()
    barrier = pltpu.get_barrier_semaphore()
    for target in (near, far):
        pl.semaphore_signal(barrier, inc=1, device_id={"mp": target}, device_id_type=mesh_id)
    others(lambda j: pl.semaphore_signal(barrier, inc=1, device_id={"dp": j}, device_id_type=mesh_id))

    source = jnp.where(place <= 1, me + 1, me - 1)
    used, heavy, left_slots = device_facts(lengths, me)
    s_used, s_heavy, s_left = device_facts(lengths, source)
    kept = jnp.where(heavy > 0, 4, used)
    wanted = []
    for b in range(4):
        wanted.append((left_slots + b, flag(b < kept)))
    for b in range(2):
        wanted.append((jnp.int32(b), heavy * flag(b < left_slots)))
    for b in range(2):
        slot = left_slots + 4 + b
        wanted.append((slot, heavy * flag(slot < used)))
    sizes = [slot_length(lengths, me, slot, valid) for slot, valid in wanted]
    own_sizes = sizes[:4]
    own_rates = [advantage[me, jnp.minimum(slot, lengths.shape[1] - 1)] for slot, _ in wanted[:4]]
    in_sizes, in_rates = [], []
    for b in range(2):
        slot = jnp.where(place <= 1, b, s_left + 4 + b)
        valid = s_heavy * jnp.where(place <= 1, flag(b < s_left), flag(slot < s_used))
        in_sizes.append(slot_length(lengths, source, slot, valid))
        in_rates.append(advantage[source, jnp.minimum(slot, lengths.shape[1] - 1)])
    block_sizes = own_sizes[:2] + [own_sizes[2 + b] + in_sizes[b] for b in range(2)]
    block_rates = own_rates[:2] + [jnp.where(in_sizes[b] > 0, in_rates[b], own_rates[2 + b]) for b in range(2)]

    row_of = lax.broadcasted_iota(jnp.int32, (BLOCK, hidden_ref.shape[0]), 0)
    ahead = lax.broadcasted_iota(jnp.int32, (BLOCK, hidden_ref.shape[0]), 1) - row_of
    for b, (slot, _) in enumerate(wanted):
        hit = (ahead == slot_start(lengths, me, slot)) & (row_of < sizes[b])
        pick_ref[b * BLOCK : (b + 1) * BLOCK] = jnp.where(hit, 1.0, 0.0).astype(jnp.bfloat16)

    pl.semaphore_wait(barrier, count + 1)

    fetches[0].wait()
    for c in range(CHUNKS):
        columns = slice(c * chunk, (c + 1) * chunk)

        @pl.when(middle)
        def _():
            both = dot32(pick_ref[CAP_L:], hidden_ref[:, columns]).astype(jnp.bfloat16)
            for side in range(2):
                piece_h[side, :, columns] = both[side * HALF : (side + 1) * HALF]
                piece_copy(side, c).start()

        full[m, :HALF, columns] = dot32(pick_ref[:HALF], hidden_ref[:, columns]).astype(jnp.bfloat16)
        over_mp(0, 1, c).start()
        over_mp(0, 0, c).start()

    for c in range(CHUNKS):
        over_mp(0, 2, c).start()
    fetches[1].wait()
    fetches[2].wait()

    def spread(rows, store):
        for base, array in ((0, query_ref), (heads, upstream_ref)):
            for at in range(0, heads, 4):
                picked = dot32(pick_ref[rows], array[:, at * HD : (at + 4) * HD]).astype(jnp.bfloat16)
                for h in range(4):
                    store(base + at + h, picked[:, h * HD : (h + 1) * HD])

    @pl.when(middle)
    def _():
        def store(h, values):
            piece_qu[0, h] = values[:HALF]
            piece_qu[1, h] = values[HALF:]

        spread(slice(CAP_L, 2 * CAP_L), store)

    @pl.when(middle)
    def _():
        for side in range(2):
            piece_copy(side, CHUNKS).start()

    def store_own(h, values):
        qu[h] = values

    def near_slices(h):
        send_slices(h, m, 0, per)
        for c in range(CHUNKS):
            over_mp(h, 0, c).wait_recv()
        send_slices(h, near, 0, per)

    spread(slice(0, CAP_L), store_own)
    fetches[3].wait()
    fetches[4].wait()

    def absorb(h, c):
        total = jnp.zeros(kv_acc.shape, jnp.float32) if c == 0 else kv_acc[...]
        squared = jnp.zeros(squares.shape, jnp.float32) if c == 0 else squares[...]
        for owner in range(owners):
            block = full[owner, h * HALF : (h + 1) * HALF, c * chunk : (c + 1) * chunk]
            spot = owner * width + c * chunk
            total += dot32(block, weight_ref[spot : spot + chunk])
            for at in range(0, chunk, HD):
                wide = block[:, at : at + HD].astype(jnp.float32)
                squared += wide * wide
        kv_acc[...] = total
        squares[...] = squared

    corner = (1 - half) * 2 + 1 - core

    def pass_first(h, c):
        over_mp(h, 1, c).wait_recv()
        over_mp(h, 3, c).start()

    def slice_first(h, c):
        over_mp(h, 3, c).wait_recv()
        first, last = finished(c)
        if last > first:
            for block in (far, corner):
                send_slices(h, block, first, last)

    def pass_rest(h):
        for c in range(CHUNKS):
            over_mp(h, 2, c).wait_recv()
            over_mp(h, 4, c).start()
            if c > 0:
                over_mp(h, 4, c - 1).wait_recv()
                absorb(h, c - 1)

    def absorb_last(h):
        over_mp(h, 4, CHUNKS - 1).wait_recv()
        absorb(h, CHUNKS - 1)

    for c in range(CHUNKS):
        columns = slice(c * chunk, (c + 1) * chunk)
        pass_first(0, c)
        own = dot32(pick_ref[HALF:CAP_L], hidden_ref[:, columns])
        piece_copy(0, c).wait_recv()
        full[m, HALF:, columns] = (own + inc_h[:, columns].astype(jnp.float32)).astype(jnp.bfloat16)
        over_mp(1, 1, c).start()
        over_mp(1, 0, c).start()
        slice_first(0, c)
    for c in range(CHUNKS):
        over_mp(1, 2, c).start()
    near_slices(0)
    pass_rest(0)
    absorb_last(0)

    def local_slice(h):
        columns = pl.ds(pl.multiple_of(me % per * share, share), share)
        slices[h, me] = full[me // per, h * HALF : (h + 1) * HALF, columns].reshape(owners, part, share)

    def attend(h):
        scale = lax.rsqrt(jnp.sum(squares[...], axis=1, keepdims=True) / (owners * width) + epsilon)
        keys_values = (kv_acc[...] * scale).astype(jnp.bfloat16)
        inverse_root = HD ** (-0.5)
        u = lax.broadcasted_iota(jnp.int32, (BLOCK, heads * BLOCK), 0)
        t = lax.broadcasted_iota(jnp.int32, (BLOCK, heads * BLOCK), 1) % BLOCK
        allowed = u <= t
        row = lax.broadcasted_iota(jnp.int32, (BLOCK, HD), 0)
        terms = []
        for b in range(2):
            block = 2 * h + b
            rows = slice(block * BLOCK, (block + 1) * BLOCK)
            key, value = (keys_values[b * BLOCK : (b + 1) * BLOCK, at : at + HD] for at in (0, HD))
            size = jnp.full((BLOCK, HD), block_sizes[block], jnp.int32)
            rate = jnp.full((BLOCK, HD), block_rates[block], jnp.float32) / jnp.maximum(size, 1).astype(jnp.float32)
            rate = jnp.where(row < size, rate, 0.0)
            query = qu[:heads, rows].reshape(heads * BLOCK, HD)
            cot = (qu[heads:, rows].astype(jnp.float32) * rate[None]).astype(jnp.bfloat16).reshape(heads * BLOCK, HD)
            scores = lax.dot_general(key, query, across, preferred_element_type=jnp.float32) * inverse_root
            scores = jnp.where(allowed, scores, masked_score)
            raised = jnp.exp(scores - jnp.max(scores, axis=0, keepdims=True))
            probability = raised * (1.0 / jnp.sum(raised, axis=0, keepdims=True))
            weights = probability.astype(jnp.bfloat16)
            attended = lax.dot_general(weights, value, down, preferred_element_type=jnp.float32).astype(jnp.bfloat16)
            for q in range(heads):
                out_buf[rows, q * HD : (q + 1) * HD] = attended[q * BLOCK : (q + 1) * BLOCK]
            prob_grad = lax.dot_general(value, cot, across, preferred_element_type=jnp.float32)
            centre = jnp.sum(probability * prob_grad, axis=0, keepdims=True)
            score_grad = (probability * (prob_grad - centre)).astype(jnp.bfloat16)
            key_cot = dot32(score_grad, query) * inverse_root
            value_cot = dot32(weights, cot)
            terms.append(jnp.concatenate([key_cot, value_cot], axis=1))
        cots = jnp.concatenate(terms, axis=0) * scale
        cots_ref[h, :, pl.ds(pl.multiple_of(me * HALF, HALF), HALF)] = cots.T.astype(jnp.bfloat16)

    attend(0)
    send_cots(0)
    near_slices(1)
    local_slice(0)

    @pl.when(gives_left)
    def _():
        out_copy(0).start()

    for c in range(CHUNKS):
        pass_first(1, c)
        if c > 0:
            slice_first(1, c - 1)
    slice_first(1, CHUNKS - 1)
    pass_rest(1)
    send_over_mp(0)
    piece_copy(0, CHUNKS).wait_recv()
    for h in range(2 * heads):
        qu[h, HALF:] = (qu[h, HALF:].astype(jnp.float32) + inc_qu[h].astype(jnp.float32)).astype(jnp.bfloat16)
    absorb_last(1)
    attend(1)
    send_cots(1)
    pass_cots(0)
    local_slice(1)

    no_left = flag(has_left) * (1 - device_facts(lengths, jnp.maximum(me - 1, 0))[1])
    sends_two = jnp.full((BLOCK, out_buf.shape[1]), no_left, jnp.int32) > 0
    out_right_buf[...] = jnp.where(
        sends_two, out_buf[HALF : HALF + BLOCK].astype(jnp.float32), out_buf[BLOCK:HALF].astype(jnp.float32)
    ).astype(jnp.bfloat16)

    @pl.when(gives_right)
    def _():
        out_copy(1).start()

    @pl.when(jnp.logical_not(takes_left))
    def _():
        out_in[:BLOCK] = jnp.zeros((BLOCK, out_in.shape[1]), jnp.bfloat16)

    @pl.when(jnp.logical_not(takes_right))
    def _():
        out_in[BLOCK:] = jnp.zeros((BLOCK, out_in.shape[1]), jnp.bfloat16)

    def one_line(j):
        for i in (j, j // 2 * 2 + 1 - side_y):
            slices_on(1, i)

    slices_on(1, partner)
    along_line(one_line)
    relay_over_mp(0)

    heavy_left = flag(has_left) * device_facts(lengths, jnp.maximum(me - 1, 0))[1]
    heavy_right = flag(has_right) * device_facts(lengths, jnp.minimum(me + 1, count - 1))[1]
    light = 1 - heavy
    gives = flag(has_left) * (1 - heavy_left)
    second = flag(me > 1) * (1 - device_facts(lengths, jnp.maximum(me - 2, 0))[1])
    from_left = light * flag(has_left) * (1 - heavy_left) * lengths[jnp.maximum(me - 1, 0), second + 1]
    from_right = light * flag(has_right) * (1 - heavy_right) * lengths[jnp.minimum(me + 1, count - 1), 0]
    total_in = in_sizes[0] + in_sizes[1]
    kept_size = lengths[me, gives]
    base_kept = from_left + heavy_left * total_in
    base_in = jnp.where(heavy_left > 0, 0, base_kept + kept_size)
    base_right = base_kept + kept_size + heavy_right * total_in
    spots = []
    running = jnp.int32(0)
    for b in range(4):
        if b < 2:
            size, at = jnp.where(gives == b, kept_size, 0), base_kept
        else:
            size, at = in_sizes[b - 2], base_in + (in_sizes[0] if b == 3 else 0)
        spots.append((jnp.where(heavy > 0, running, at), jnp.where(heavy > 0, own_sizes[b], size)))
        running = running + own_sizes[b]
    spots += [(jnp.int32(0), from_left), (base_right, from_right)]
    target = lax.broadcasted_iota(jnp.int32, (CAP_L, HALF), 0)
    lane = lax.broadcasted_iota(jnp.int32, (CAP_L, HALF), 1)
    first = lane < BLOCK
    offset = lane % BLOCK
    for pair in range(3):
        (at0, size0), (at1, size1) = spots[2 * pair : 2 * pair + 2]
        at = jnp.where(first, at0, at1)
        size = jnp.where(first, size0, size1)
        hit = (target - at == offset) & (offset < size)
        place_ref[:, pair * HALF : (pair + 1) * HALF] = jnp.where(hit, 1.0, 0.0).astype(jnp.bfloat16)

    def place_out():
        @pl.when(takes_left)
        def _():
            out_copy(1).wait_recv()

        @pl.when(takes_right)
        def _():
            out_copy(0).wait_recv()

        for at in range(0, out_ref.shape[1], 256):
            columns = slice(at, at + 256)
            total = dot32(place_ref[:, :CAP_L], out_buf[:, columns]) + dot32(place_ref[:, CAP_L:], out_in[:, columns])
            out_ref[:, columns] = total.astype(jnp.bfloat16)

    for h in range(2):
        if h == 1:
            relay_over_mp(1)
            place_out()

        def gathered(i):
            slices_mp(h, 0, i).wait_recv()
            slices_mp(h, 2, i).wait_recv()

        others(gathered)
        if h == 1:
            others(lambda j: cot_on(h, j).wait_recv())
        else:
            cot_on(h, partner).wait_recv()
            along_line(lambda j: cot_on(h, j // 2 * 2 + 1 - side_y).wait_recv())
        tile = min(256, share)
        for at in range(0, share, tile):
            columns = slice(at, at + tile)
            rows = slices[h, :, :, :, columns].reshape(count * HALF, tile)
            term = dot32(cots_ref[h], rows)
            if h == 0:
                acc[:, columns] = term
            else:
                acc[:, columns] += term
    key_grad_ref[...] = acc[:HD].T
    value_grad_ref[...] = acc[HD:].T

    @pl.when(middle)
    def _():
        for side in range(2):
            for p in range(CHUNKS + 1):
                piece_copy(side, p).wait_send()

    @pl.when(gives_left)
    def _():
        out_copy(0).wait_send()

    @pl.when(gives_right)
    def _():
        out_copy(1).wait_send()

    for h in range(2):
        for kind in range(5):
            for c in range(CHUNKS):
                over_mp(h, kind, c).wait_send()

        def left(j):
            slice_out(h, j).wait_send()
            for kind in range(3):
                slices_mp(h, kind, j).wait_send()

        def passed(j):
            cot_out(h, j).wait_send()
            cot_on(h, j).wait_send()

        others(left)
        if h == 1:
            others(lambda j: cot_out(h, j).wait_send())
        else:
            along_line(passed)
            cot_out(h, partner).wait_send()


def write_kernel(*refs):
    inputs, outputs, done = refs[:3], refs[3:6], refs[6]
    copies = [pltpu.make_async_copy(a, b, done.at[n]) for n, (a, b) in enumerate(zip(inputs, outputs))]
    for copy in copies:
        copy.start()
    for copy in copies:
        copy.wait()


def write_out(*arrays):
    return pl.pallas_call(
        write_kernel,
        in_specs=[pl.BlockSpec(memory_space=pltpu.VMEM)] * 3,
        out_specs=[pl.BlockSpec(memory_space=pltpu.HBM)] * 3,
        out_shape=[jax.ShapeDtypeStruct(array.shape, array.dtype) for array in arrays],
        scratch_shapes=[pltpu.SemaphoreType.DMA((3,))],
        compiler_params=pltpu.CompilerParams(vmem_limit_bytes=8 * 1024 * 1024),
    )(*arrays)


def body(hidden, queries, upstream, key_weight, value_weight, lengths, advantage):
    count, owners = lax.axis_size("dp"), lax.axis_size("mp")
    rows, width = hidden.shape
    head_width = queries.shape[1]
    heads = head_width // HD
    depth = key_weight.shape[0]
    share = depth // count
    vmem = pl.BlockSpec(memory_space=pltpu.VMEM)
    smem = pl.BlockSpec(memory_space=pltpu.SMEM)
    bf16 = lambda *shape: pltpu.VMEM(shape, jnp.bfloat16)
    f32 = lambda *shape: pltpu.VMEM(shape, jnp.float32)
    sems = lambda *shape: pltpu.SemaphoreType.DMA(shape)
    results = pl.pallas_call(
        functools.partial(fused_kernel, count),
        in_specs=[smem] * 2 + [pl.BlockSpec(memory_space=pl.ANY)] * 5,
        out_specs=[vmem] * 3,
        out_shape=[
            jax.ShapeDtypeStruct((CAP_L, head_width), jnp.bfloat16),
            jax.ShapeDtypeStruct((share, HD), jnp.float32),
            jax.ShapeDtypeStruct((share, HD), jnp.float32),
        ],
        scratch_shapes=[
            bf16(rows, width), bf16(rows, head_width), bf16(rows, head_width), bf16(depth, 2 * HD),
            bf16(8 * BLOCK, rows), bf16(CAP_L, CAP_L + HALF),
            bf16(2, HALF, width), bf16(2, 2 * heads, HALF, HD), bf16(HALF, width), bf16(2 * heads, HALF, HD),
            bf16(owners, CAP_L, width), bf16(2 * heads, CAP_L, HD), f32(HALF, 2 * HD), f32(HALF, HD),
            bf16(CAP_L, head_width), bf16(BLOCK, head_width), bf16(HALF, head_width),
            bf16(2, 2 * HD, count * HALF), bf16(2, count, owners, HALF // owners, share), f32(2 * HD, share),
            sems(5), sems(2, CHUNKS + 1), sems(CHUNKS + 1), sems(2, 5, CHUNKS), sems(2, 5, CHUNKS),
            sems(2, count), sems(2, count), sems(2, 3, count), sems(2, 3, count),
            sems(2, count), sems(2, count), sems(2, count), sems(2), sems(2),
        ],
        compiler_params=pltpu.CompilerParams(
            collective_id=0, has_side_effects=True, vmem_limit_bytes=40 * 1024 * 1024
        ),
    )(*(
        pltpu.with_memory_space_constraint(array, pltpu.HBM)
        for array in (lengths, advantage, hidden, queries, upstream, key_weight, value_weight)
    ))
    return tuple(write_out(*results))


def solution(mesh):
    in_specs = (P("dp", "mp"), P("dp", "mp"), P("dp", "mp"), P(None, "mp"), P(None, "mp"), P(), P())
    out_specs = (P("dp", "mp"), P("dp", "mp"), P("dp", "mp"))
    return jax.shard_map(body, mesh=mesh, in_specs=in_specs, out_specs=out_specs, check_vma=False)
```
